32 devices in a mesh: gx: 4 (over z), gy: 2 (over x), ka: 4 (over y, core).
Axes of the slice: x: 2, y: 2, z: 4, core: 2. Of those that a mesh axis runs over, the one named last changes fastest.
Arguments:
- band_fields: bfloat16 [4, 2, 3, 8, 8, 128, 128], P('ka', None, None, None, 'gx', 'gy'), may hold values from -400 to 400
- labels: int32 [8, 128, 128], P('gx', 'gy'), may hold values from 0 to 2
- phase_props: float32 [3, 3], replicated, may hold values from 0.5 to 4
- slopes: float32 [3, 3], replicated, may hold values from -1 to 1
- kpoints: int32 [4], P('ka'), may hold values from 0 to 511
- rotations: float32 [4, 2, 8, 8], P('ka'), may hold values from -1.5 to 1.5
- band_weights: float32 [4, 8], P('ka'), may hold values from -0.06 to 0.06
Outputs:
- ritz_values: float32 [4, 8], P('ka')
- design_grad: float32 [8, 128, 128], P('gx', ('gy', 'ka'))
The draws below stay inside these ranges and needn't reach their ends.
All inputs are finite; a program needn't handle non-finite values.
Results may differ from the reference program's by a relative error of at most 0.0003.
Values may be sent and summed in bfloat16 or wider, within the bound.
No kernel may reach another device: no remote copies, remote signals or barrier semaphores. Data moves between devices by JAX's collectives and lax.ppermute only.
A program may use at most 256 MiB of HBM per device.

```python
import math
import jax
import jax.numpy as jnp
from jax import lax

BANDS = 8
NZ = 128
QGRID = 8
PHASES = 3
KPTS = 4
NX = 8
NY = 128


def draw_band_fields(key, part):
    dims_all = (KPTS, 2, 3, BANDS, NX, NY, NZ)
    noise_key = jax.random.fold_in(key, 11)
    scale_key = jax.random.fold_in(key, 12)
    noise_draw = jnp.clip(jax.random.normal(noise_key, dims_all, jnp.float32), -6.0, 6.0)
    ramp_rate = 0.8
    cell_scale = jnp.exp(jax.random.uniform(scale_key, (NX, NY, NZ), jnp.float32, 0.0, 0.5 * math.log(10.0)))
    x_ramp = 1.0 + ramp_rate * jnp.arange(NX, dtype=jnp.float32) / NX
    y_ramp = 1.0 + ramp_rate * jnp.arange(NY, dtype=jnp.float32) / NY
    amplitude = cell_scale * x_ramp[:, None, None] * y_ramp[None, :, None]
    return (noise_draw * amplitude).astype(jnp.bfloat16)


def draw_labels(key, part):
    levels = jax.random.randint(key, (NX, NY, NZ), 0, 1000)
    x_pos = jnp.arange(NX, dtype=jnp.int32)[:, None, None]
    y_pos = jnp.arange(NY, dtype=jnp.int32)[None, :, None]
    low_cut = 100 + 400 * x_pos // NX + 200 * y_pos // NY
    high_cut = low_cut + 250
    return (levels >= low_cut).astype(jnp.int32) + (levels >= high_cut).astype(jnp.int32)


def set_ends(array, rng, least, high):
    dims = array.shape
    spot = [jax.random.randint(jax.random.fold_in(rng, axis), (), 0, dims[axis]) for axis in range(len(dims))]
    array = array.at[tuple(spot)].set(least)
    longest = dims.index(max(dims))
    spot[longest] = (spot[longest] + 1) % dims[longest]
    return array.at[tuple(spot)].set(high)


def block_scale(stream_key, shape, split, least, top_value):
    def one(axis_at, shards_of):
        heights = jax.random.uniform(jax.random.fold_in(jax.random.fold_in(stream_key, 6), axis_at), (shards_of,), jnp.float32, least / len(split), top_value / len(split))
        return jnp.repeat(jnp.exp(heights), shape[axis_at] // shards_of).reshape((-1,) + (1,) * (len(shape) - axis_at - 1))

    gain = one(*split[0])
    for cut in split[1:]:
        gain = gain * one(*cut)
    return gain


def centred(rng, extent, spread, most, split=(), held_as=jnp.bfloat16):
    level = block_scale(rng, extent, split, -0.22, 0.18) if split else 1.0
    array = jax.random.normal(rng, extent, jnp.float32) * spread * level
    return jnp.minimum(jnp.maximum(array, -most), most).astype(held_as)


def setup_inputs(seed: int = 0) -> dict:
    keys = jax.random.split(jax.random.key(seed), 8)
    band_fields = draw_band_fields(jax.random.fold_in(keys[7], 71), 0)
    labels = draw_labels(jax.random.fold_in(keys[7], 71), 0)
    phase_props = jnp.clip(jnp.exp(jax.random.uniform(keys[2], (PHASES, 3), jnp.float32, math.log(0.5), math.log(4.0))), 0.5, 4.0)
    slopes = jnp.clip(jax.random.uniform(keys[3], (PHASES, 3), jnp.float32, -1.0, 1.0), -1.0, 1.0)
    kpoints = set_ends(jax.random.randint(keys[4], (KPTS,), 0, QGRID ** 3), jax.random.fold_in(keys[4], 1), 0, (QGRID ** 3) - 1).astype(jnp.int32)
    rotations = centred(keys[5], (KPTS, 2, BANDS, BANDS), (2 * BANDS) ** -0.5, 1.5, ((0, 4),), jnp.float32)
    band_weights = jnp.clip(jax.random.uniform(keys[6], (KPTS, BANDS), jnp.float32, -0.06, 0.06) * block_scale(keys[6], (KPTS, BANDS), ((0, 4),), -0.4, 0.0), -0.06, 0.06)
    return {"band_fields": band_fields, "labels": labels, "phase_props": phase_props, "slopes": slopes, "kpoints": kpoints, "rotations": rotations, "band_weights": band_weights}


exact_mode = lax.Precision.HIGHEST


def turn_phase(source, cosine_part, sine_part):
    return jnp.stack([cosine_part * source[0] - sine_part * source[1],
                      sine_part * source[0] + cosine_part * source[1]])


def advance(source, direction, cosine_part, sine_part):
    first_plane = lax.slice_in_dim(source, 0, 1, axis=direction)
    remainder = lax.slice_in_dim(source, 1, source.shape[direction], axis=direction)
    return jnp.concatenate([remainder, turn_phase(first_plane, cosine_part, sine_part)], axis=direction)


def rotation_block(rotation):
    real_part = rotation[0]
    imag_part = rotation[1]
    return jnp.stack([jnp.stack([real_part, imag_part], axis=1),
                      jnp.stack([-imag_part, real_part], axis=1)], axis=0)


def wave_angles(wave_index):
    digits = jnp.stack([wave_index // (QGRID * QGRID), (wave_index // QGRID) % QGRID, wave_index % QGRID])
    return digits.astype(jnp.float32) * (2.0 * math.pi / QGRID)


def material(lookup_table, column, label_block):
    phase_ids = jnp.arange(PHASES, dtype=jnp.int32)
    onehot = (label_block[None] == phase_ids[:, None, None, None]).astype(jnp.float32)
    return jnp.sum(onehot * lookup_table[:, column][:, None, None, None], axis=0)


def reference(band_fields, labels, phase_props, slopes, kpoints, rotations, band_weights):
    shear = material(phase_props, 0, labels)
    lame = material(phase_props, 1, labels)
    density = material(phase_props, 2, labels)
    slope_s = material(slopes, 0, labels)
    slope_l = material(slopes, 1, labels)
    slope_d = material(slopes, 2, labels)
    cell_count = NX * NY * NZ

    def per_wave(accrued, inputs):
        waves, wave_index, rotation, weights = inputs
        widened = waves.astype(jnp.float32)
        angles = wave_angles(wave_index)
        cosine_part = jnp.cos(angles)
        sine_part = jnp.sin(angles)
        columns = jnp.transpose(rotation_block(rotation), (3, 0, 1, 2))

        def per_band(running, item):
            column, weight = item
            rotated = jnp.einsum('scaxyz,sat->tcxyz', widened, column, precision=exact_mode)
            strain_sq = jnp.zeros(rotated.shape[2:], jnp.float32)
            dilation = jnp.zeros((2,) + rotated.shape[2:], jnp.float32)
            for direction in range(3):
                strain = advance(rotated, direction + 2, cosine_part[direction], sine_part[direction]) - rotated
                strain_sq = strain_sq + jnp.sum(strain * strain, axis=(0, 1))
                dilation = dilation + strain[:, direction]
            dilation_sq = jnp.sum(dilation * dilation, axis=0)
            mass_sq = jnp.sum(rotated * rotated, axis=(0, 1))
            stiffness = jnp.sum(shear * strain_sq + lame * dilation_sq) / cell_count
            inertia = jnp.sum(density * mass_sq) / cell_count
            ritz_value = stiffness / inertia
            factor = weight / inertia
            running = running + factor * (slope_s * strain_sq + slope_l * dilation_sq - slope_d * ritz_value * mass_sq)
            return running, ritz_value

        accrued, values = lax.scan(per_band, accrued, (columns, weights))
        return accrued, values

    gradient, ritz_values = lax.scan(per_wave, jnp.zeros((NX, NY, NZ), jnp.float32),
                                     (band_fields, kpoints, rotations, band_weights))
    return ritz_values, gradient
```

```python
import math

import jax
import jax.numpy as jnp
from jax import lax
from jax.experimental import pallas as pl
from jax.experimental.pallas import tpu as pltpu
from jax.sharding import PartitionSpec as P

QGRID = 8
PHASES = 3
COMPS = 3
ROWS = 16
F32 = jnp.float32
BF16 = jnp.bfloat16
VMEM_LIMIT = 56 * 1024 * 1024

vmem = pl.BlockSpec(memory_space=pltpu.VMEM)
smem = pl.BlockSpec(memory_space=pltpu.SMEM)


def passed_along(value, axis, by):
    devices = lax.axis_size(axis)
    return lax.ppermute(value, axis, [(i, (i + by) % devices) for i in range(devices)])


def swapped(value, axis, flip):
    devices = lax.axis_size(axis)
    return lax.ppermute(value, axis, [(i, i ^ flip) for i in range(devices)])


def is_power(count):
    return count & (count - 1) == 0


def wave_angles(wave_index):
    digits = jnp.stack(
        [wave_index // (QGRID * QGRID), wave_index // QGRID % QGRID, wave_index % QGRID]
    )
    return digits.astype(F32) * (2.0 * math.pi / QGRID)


def mixing_rows(real_part, imag_part):
    top = jnp.concatenate([real_part.T, -imag_part.T], axis=1)
    bottom = jnp.concatenate([imag_part.T, real_part.T], axis=1)
    return jnp.concatenate([top, bottom], axis=0)


def bf16_parts(value):
    high = value.astype(BF16)
    rest = value - high.astype(F32)
    middle = rest.astype(BF16)
    low = (rest - middle.astype(F32)).astype(BF16)
    return [high, middle, low]


def spread_rotation(mixing, channels):
    wide = channels * ROWS
    tall_iota = lax.broadcasted_iota(jnp.int32, (wide, channels), 0) // ROWS
    tall = (tall_iota == lax.broadcasted_iota(jnp.int32, (wide, channels), 1)).astype(BF16)
    flat_iota = lax.broadcasted_iota(jnp.int32, (channels, wide), 1) // ROWS
    flat = (flat_iota == lax.broadcasted_iota(jnp.int32, (channels, wide), 0)).astype(BF16)
    same_row = (lax.broadcasted_iota(jnp.int32, (wide, wide), 0) % ROWS) == (
        lax.broadcasted_iota(jnp.int32, (wide, wide), 1) % ROWS
    )
    blocks = []
    for part in bf16_parts(mixing):
        rows = jnp.dot(tall, part, preferred_element_type=F32).astype(BF16)
        full = jnp.dot(rows, flat, preferred_element_type=F32)
        blocks.append(jnp.where(same_row, full, 0.0).astype(BF16))
    return jnp.concatenate(blocks, axis=1)


def picked(table, column, label_block):
    low = jnp.where(label_block == 0, table[0, column], table[1, column])
    return jnp.where(label_block == 2, table[2, column], low)


def interior_kernel(
    mix_ref,
    turn_ref,
    props_ref,
    slopes_ref,
    labels_ref,
    u_ref,
    yrow_ref,
    spread_ref,
    last_modes_ref,
    grad_ref,
    massd_ref,
    strain_ref,
    dil_ref,
    sums_ref,
    modes_ref,
    mats_ref,
    acc_ref,
):
    planes, rows, lanes = labels_ref.shape
    bands = u_ref.shape[2]
    channels = 2 * bands
    spread_own = spread_rotation(mix_ref[0], channels)
    spread_ref[...] = spread_rotation(mix_ref[1], channels)
    edge_mix = jnp.concatenate(bf16_parts(mix_ref[2]), axis=1)
    for tile in range(rows // ROWS):
        here = slice(tile * ROWS, (tile + 1) * ROWS)
        for comp in range(COMPS):
            source = jnp.concatenate(
                [
                    u_ref[:, comp, :, plane, here, :].reshape(channels * ROWS, lanes)
                    for plane in range(planes)
                ],
                axis=1,
            )
            source = jnp.concatenate([source] * 3, axis=0)
            turned = jnp.dot(spread_own, source, preferred_element_type=F32)
            for plane in range(planes):
                part = turned[:, plane * lanes : (plane + 1) * lanes]
                part = part.reshape(channels, ROWS, lanes)
                modes_ref[plane, comp, :, here, :] = part
                if plane == planes - 1:
                    last_modes_ref[comp, :, here, :] = part
    for plane in range(planes):
        for comp in range(COMPS):
            edge = yrow_ref[comp, plane]
            edge = jnp.concatenate([edge] * 3, axis=0)
            edge = jnp.dot(edge_mix, edge, preferred_element_type=F32)
            modes_ref[plane, comp, :, rows : rows + 1, :] = edge[:, None, :]
        for column in range(3):
            mats_ref[column, plane] = picked(props_ref, column, labels_ref[plane])
            mats_ref[3 + column, plane] = picked(slopes_ref, column, labels_ref[plane])
    lane_at = lax.broadcasted_iota(jnp.int32, (ROWS, lanes), 1)
    is_end = lane_at == lanes - 1
    turn_cos = jnp.where(is_end, turn_ref[0], 1.0)
    turn_sin = jnp.where(is_end, turn_ref[1], 0.0)

    def per_band(band, carry):
        for plane in range(planes):
            inner = plane < planes - 1
            mass_sum = jnp.zeros((ROWS, lanes), F32)
            stiff_sum = jnp.zeros((ROWS, lanes), F32)
            for tile in range(rows // ROWS):
                begin = tile * ROWS
                here = slice(begin, begin + ROWS)
                after = slice(begin + 1, begin + 1 + ROWS)
                strain_sq = jnp.zeros((ROWS, lanes), F32)
                mass_sq = jnp.zeros((ROWS, lanes), F32)
                dil = [jnp.zeros((ROWS, lanes), F32)] * 2
                for comp in range(COMPS):
                    own = [modes_ref[plane, comp, t * bands + band, here, :] for t in range(2)]
                    roll = [pltpu.roll(v, lanes - 1, 1) for v in own]
                    along_z = [
                        turn_cos * roll[0] - turn_sin * roll[1],
                        turn_sin * roll[0] + turn_cos * roll[1],
                    ]
                    for t in range(2):
                        diff_z = along_z[t] - own[t]
                        diff_y = modes_ref[plane, comp, t * bands + band, after, :] - own[t]
                        strain_sq = strain_sq + diff_z * diff_z + diff_y * diff_y
                        if inner:
                            diff_x = (
                                modes_ref[plane + 1, comp, t * bands + band, here, :] - own[t]
                            )
                            strain_sq = strain_sq + diff_x * diff_x
                            if comp == 0:
                                dil[t] = dil[t] + diff_x
                        if comp == 1:
                            dil[t] = dil[t] + diff_y
                        if comp == 2:
                            dil[t] = dil[t] + diff_z
                        mass_sq = mass_sq + own[t] * own[t]
                mass_sum = mass_sum + mats_ref[2, plane, here, :] * mass_sq
                massd_ref[band, plane, here, :] = mats_ref[5, plane, here, :] * mass_sq
                if inner:
                    dil_sq = dil[0] * dil[0] + dil[1] * dil[1]
                    stiff_sum = (
                        stiff_sum
                        + mats_ref[0, plane, here, :] * strain_sq
                        + mats_ref[1, plane, here, :] * dil_sq
                    )
                    grad_ref[band, plane, here, :] = (
                        mats_ref[3, plane, here, :] * strain_sq
                        + mats_ref[4, plane, here, :] * dil_sq
                    )
                else:
                    strain_ref[band, here, :] = strain_sq
                    dil_ref[0, band, here, :] = dil[0]
                    dil_ref[1, band, here, :] = dil[1]
            acc_ref[plane, band] = stiff_sum
            acc_ref[planes + plane, band] = mass_sum
        return carry

    lax.fori_loop(0, bands, per_band, 0)
    sums_ref[0:bands] = jnp.sum(jnp.sum(acc_ref[0:planes], axis=0), axis=1)
    sums_ref[bands : 2 * bands] = jnp.sum(jnp.sum(acc_ref[planes : 2 * planes], axis=0), axis=1)


def edge_kernel(
    props_ref,
    slopes_ref,
    labels_ref,
    xplane_ref,
    spread_ref,
    last_modes_ref,
    strain_ref,
    dil_ref,
    sums_in_ref,
    grad_ref,
    sums_ref,
    next_ref,
    acc_ref,
):
    rows, lanes = labels_ref.shape[1:]
    bands = xplane_ref.shape[2]
    channels = 2 * bands
    spread = spread_ref[...]
    label_block = labels_ref[labels_ref.shape[0] - 1]
    mats = [picked(table, column, label_block) for table in (props_ref, slopes_ref) for column in (0, 1)]
    for tile in range(rows // ROWS):
        here = slice(tile * ROWS, (tile + 1) * ROWS)
        for comp in range(COMPS):
            source = xplane_ref[:, comp, :, here, :].reshape(channels * ROWS, lanes)
            source = jnp.concatenate([source] * 3, axis=0)
            turned = jnp.dot(spread, source, preferred_element_type=F32)
            next_ref[comp, :, here, :] = turned.reshape(channels, ROWS, lanes)

    for band in range(bands):
        stiff_sum = jnp.zeros((ROWS, lanes), F32)
        for tile in range(rows // ROWS):
            here = slice(tile * ROWS, (tile + 1) * ROWS)
            strain_sq = strain_ref[band, here, :]
            dil = [dil_ref[t, band, here, :] for t in range(2)]
            for comp in range(COMPS):
                for t in range(2):
                    diff_x = (
                        next_ref[comp, t * bands + band, here, :]
                        - last_modes_ref[comp, t * bands + band, here, :]
                    )
                    strain_sq = strain_sq + diff_x * diff_x
                    if comp == 0:
                        dil[t] = dil[t] + diff_x
            dil_sq = dil[0] * dil[0] + dil[1] * dil[1]
            stiff_sum = stiff_sum + mats[0][here] * strain_sq + mats[1][here] * dil_sq
            grad_ref[band, here, :] = mats[2][here] * strain_sq + mats[3][here] * dil_sq
        acc_ref[band] = stiff_sum
    sums_ref[0:bands] = sums_in_ref[0:bands] + jnp.sum(acc_ref[...], axis=1)
    sums_ref[bands : 2 * bands] = sums_in_ref[bands : 2 * bands]


def make_combine_kernel(cell_count, slabs):
    def combine_kernel(
        order_ref, weights_ref, sums_a_ref, sums_b_ref, grad_ref, last_grad_ref, massd_ref, ritz_ref, *slab_refs
    ):
        bands, planes, rows, lanes = massd_ref.shape
        sums = jnp.sum(sums_a_ref[...] + sums_b_ref[...], axis=1, keepdims=True)
        sums = jnp.broadcast_to(sums, (2 * bands, lanes))
        stiff = sums[0:bands]
        inert = sums[bands : 2 * bands]
        ritz = stiff / inert
        factor = weights_ref[...] * (cell_count / inert)
        tail = factor * ritz
        diagonal = lax.broadcasted_iota(jnp.int32, (bands, lanes), 0) == lax.broadcasted_iota(
            jnp.int32, (bands, lanes), 1
        )
        ritz_row = jnp.sum(jnp.where(diagonal, ritz, 0.0), axis=0, keepdims=True)
        ritz_ref[...] = ritz_row[:, 0:bands]
        size = rows // slabs
        for at in range(slabs):
            begin = pl.multiple_of(order_ref[at] * size, size)
            for plane in range(planes):
                total = jnp.zeros((size, lanes), F32)
                for band in range(bands):
                    if plane < planes - 1:
                        term = grad_ref[band, plane, pl.ds(begin, size), :]
                    else:
                        term = last_grad_ref[band, pl.ds(begin, size), :]
                    total = total + factor[band : band + 1] * term
                    total = total - tail[band : band + 1] * massd_ref[band, plane, pl.ds(begin, size), :]
                slab_refs[at][plane] = total

    return combine_kernel


def on_device(band_fields, labels, phase_props, slopes, kpoints, rotations, band_weights):
    waves = band_fields[0]
    planes, rows, lanes = labels.shape
    bands = waves.shape[2]
    channels = 2 * bands
    gx_size = lax.axis_size("gx")
    gy_size = lax.axis_size("gy")
    ka_size = lax.axis_size("ka")
    cell_count = gx_size * gy_size * planes * rows * lanes

    xplane = passed_along(waves[:, :, :, 0], "gx", -1)
    yrow = waves[:, :, :, :, 0, :].transpose(1, 3, 0, 2, 4).reshape(COMPS, planes, channels, lanes)
    yrow = passed_along(yrow, "gy", -1)

    angles = wave_angles(kpoints[0])
    cosine = jnp.cos(angles)
    sine = jnp.sin(angles)
    x_last = lax.axis_index("gx") == gx_size - 1
    y_last = lax.axis_index("gy") == gy_size - 1
    real_part, imag_part = rotations[0, 0], rotations[0, 1]
    mixes = [mixing_rows(real_part, imag_part)]
    for axis, is_last in ((0, x_last), (1, y_last)):
        turn_cos = jnp.where(is_last, cosine[axis], 1.0)
        turn_sin = jnp.where(is_last, sine[axis], 0.0)
        mixes.append(
            mixing_rows(
                real_part * turn_cos - imag_part * turn_sin,
                real_part * turn_sin + imag_part * turn_cos,
            )
        )
    mixes = jnp.stack(mixes)
    turn = jnp.stack([cosine[2], sine[2]])
    params = pltpu.CompilerParams(vmem_limit_bytes=VMEM_LIMIT)

    spread, last_modes, grad, massd, strain, dil, sums = pl.pallas_call(
        interior_kernel,
        out_shape=(
            jax.ShapeDtypeStruct((channels * ROWS, 3 * channels * ROWS), BF16),
            jax.ShapeDtypeStruct((COMPS, channels, rows, lanes), F32),
            jax.ShapeDtypeStruct((bands, planes - 1, rows, lanes), F32),
            jax.ShapeDtypeStruct((bands, planes, rows, lanes), F32),
            jax.ShapeDtypeStruct((bands, rows, lanes), F32),
            jax.ShapeDtypeStruct((2, bands, rows, lanes), F32),
            jax.ShapeDtypeStruct((2 * bands, lanes), F32),
        ),
        in_specs=[vmem, smem, smem, smem, vmem, vmem, vmem],
        out_specs=(vmem,) * 7,
        scratch_shapes=[
            pltpu.VMEM((planes, COMPS, channels, rows + 8, lanes), F32),
            pltpu.VMEM((6, planes, rows, lanes), F32),
            pltpu.VMEM((2 * planes, bands, ROWS, lanes), F32),
        ],
        compiler_params=params,
        name="interior",
    )(mixes, turn, phase_props, slopes, labels, waves, yrow)

    last_grad, sums = pl.pallas_call(
        edge_kernel,
        out_shape=(
            jax.ShapeDtypeStruct((bands, rows, lanes), F32),
            jax.ShapeDtypeStruct((2 * bands, lanes), F32),
        ),
        in_specs=[smem, smem] + [vmem] * 7,
        out_specs=(vmem, vmem),
        scratch_shapes=[
            pltpu.VMEM((COMPS, channels, rows, lanes), F32),
            pltpu.VMEM((bands, ROWS, lanes), F32),
        ],
        compiler_params=params,
        name="edge",
    )(phase_props, slopes, labels, xplane, spread, last_modes, strain, dil, sums)

    if is_power(gx_size) and is_power(gy_size) and gx_size > 1:
        steps = [("gy", 1 << i) for i in range(gy_size.bit_length() - 1)]
        steps += [("gx", 1 << i) for i in range(gx_size.bit_length() - 1)]
        for axis, flip in steps[:-1]:
            sums = sums + swapped(sums, axis, flip)
        other = swapped(sums, *steps[-1])
    else:
        sums = lax.psum(sums, ("gx", "gy"))
        other = jnp.zeros_like(sums)

    direct = ka_size <= 4 and rows % (8 * ka_size) == 0
    slabs = ka_size if direct else 1
    me = lax.axis_index("ka")
    order = (me + jnp.arange(slabs, dtype=jnp.int32)) % slabs
    weights = jnp.broadcast_to(band_weights[0][:, None], (bands, lanes))
    ritz, *pieces = pl.pallas_call(
        make_combine_kernel(float(cell_count), slabs),
        out_shape=(jax.ShapeDtypeStruct((1, bands), F32),)
        + (jax.ShapeDtypeStruct((planes, rows // slabs, lanes), F32),) * slabs,
        in_specs=[smem] + [vmem] * 6,
        out_specs=(vmem,) * (1 + slabs),
        compiler_params=params,
        name="combine",
    )(order, weights, sums, other, grad, last_grad, massd)
    if direct:
        design = pieces[0]
        arrived = [passed_along(pieces[hop], "ka", hop) for hop in range(1, slabs)]
        for piece in arrived:
            design = design + piece
    else:
        design = lax.psum_scatter(pieces[0], "ka", scatter_dimension=1, tiled=True)
    return (ritz, design)


def solution(mesh):
    in_specs = (
        P("ka", None, None, None, "gx", "gy", None),
        P("gx", "gy", None),
        P(),
        P(),
        P("ka"),
        P("ka", None, None, None),
        P("ka", None),
    )
    out_specs = (P("ka", None), P("gx", ("gy", "ka"), None))
    return jax.shard_map(
        on_device, mesh=mesh, in_specs=in_specs, out_specs=out_specs, check_vma=False
    )
```

```python
import math

import jax
import jax.numpy as jnp
import numpy as np
from jax import lax
from jax.experimental import pallas as pl
from jax.experimental.pallas import tpu as pltpu
from jax.sharding import PartitionSpec as P

QGRID = 8
PHASES = 3
COMPS = 3
ROWS = 16
F32 = jnp.float32
BF16 = jnp.bfloat16
EXACT = lax.Precision.HIGHEST
VMEM_LIMIT = 56 * 1024 * 1024

vmem = pl.BlockSpec(memory_space=pltpu.VMEM)
smem = pl.BlockSpec(memory_space=pltpu.SMEM)


def in_vmem(value):
    return pltpu.with_memory_space_constraint(value, pltpu.VMEM)


def passed_along(value, axis, by):
    devices = lax.axis_size(axis)
    return lax.ppermute(value, axis, [(i, (i + by) % devices) for i in range(devices)])


def swapped(value, axis, flip):
    devices = lax.axis_size(axis)
    return lax.ppermute(value, axis, [(i, i ^ flip) for i in range(devices)])


def is_power(count):
    return count & (count - 1) == 0


def grid_turn(digit):
    angles = np.arange(QGRID, dtype=np.float32) * np.float32(2.0 * math.pi / QGRID)
    cosine, sine = jnp.float32(1.0), jnp.float32(0.0)
    for at in range(1, QGRID):
        cosine = jnp.where(digit == at, jnp.float32(np.cos(angles[at])), cosine)
        sine = jnp.where(digit == at, jnp.float32(np.sin(angles[at])), sine)
    return cosine, sine


def bf16_parts(value):
    high = value.astype(BF16)
    rest = value - high.astype(F32)
    middle = rest.astype(BF16)
    low = (rest - middle.astype(F32)).astype(BF16)
    return [high, middle, low]


def spread_rotation(real_part, imag_part, rows):
    bands = real_part.shape[0]
    wide = 2 * bands * rows
    tall_at = lax.broadcasted_iota(jnp.int32, (wide, bands), 0) // rows % bands
    tall = (tall_at == lax.broadcasted_iota(jnp.int32, (wide, bands), 1)).astype(F32)
    flat_at = lax.broadcasted_iota(jnp.int32, (bands, wide), 1) // rows % bands
    flat = (flat_at == lax.broadcasted_iota(jnp.int32, (bands, wide), 0)).astype(F32)

    def grown(matrix):
        tall_part = lax.dot_general(
            tall, matrix, (((1,), (1,)), ((), ())), precision=EXACT, preferred_element_type=F32
        )
        return jnp.dot(tall_part, flat, precision=EXACT, preferred_element_type=F32)

    row_at = lax.broadcasted_iota(jnp.int32, (wide, wide), 0)
    column_at = lax.broadcasted_iota(jnp.int32, (wide, wide), 1)
    row_half = row_at // (bands * rows)
    column_half = column_at // (bands * rows)
    real_grown = grown(real_part)
    imag_grown = grown(imag_part)
    imag_grown = jnp.where(row_half > column_half, imag_grown, -imag_grown)
    full = jnp.where(row_half == column_half, real_grown, imag_grown)
    full = jnp.where(row_at % rows == column_at % rows, full, 0.0)
    return jnp.concatenate(bf16_parts(full), axis=1)


def turned_parts(real_part, imag_part, cosine, sine):
    return cosine * real_part - sine * imag_part, sine * real_part + cosine * imag_part


def picked(table, column, label_block):
    low = jnp.where(label_block == 0, table[0, column], table[1, column])
    return jnp.where(label_block == 2, table[2, column], low)


def make_slice_kernel(comp):
    def slice_kernel(u_ref, *refs):
        out_ref, sem = refs[-2:]
        copy = pltpu.make_async_copy(u_ref.at[0, :, comp, :, 0], out_ref, sem)
        copy.start()
        copy.wait()

    return slice_kernel


def edge_row_kernel(u_ref, after_ref, out_ref):
    planes = u_ref.shape[4]
    for comp in range(COMPS):
        for plane in range(planes):
            rows = u_ref[0, :, comp, :, plane, 0:1, :]
            out_ref[comp, plane] = rows.reshape(rows.shape[0] * rows.shape[1], rows.shape[3])


def interior_kernel(
    kpoint_ref,
    props_ref,
    slopes_ref,
    rotation_ref,
    labels_ref,
    u_ref,
    yrow_ref,
    spread_ref,
    last_modes_ref,
    grad_ref,
    massd_ref,
    strain_ref,
    dil_ref,
    sums_ref,
    mats_ref,
    modes_ref,
    acc_ref,
):
    planes, rows, lanes = labels_ref.shape
    bands = u_ref.shape[3]
    channels = 2 * bands
    q_index = kpoint_ref[0]
    x_last = lax.axis_index("gx") == lax.axis_size("gx") - 1
    y_last = lax.axis_index("gy") == lax.axis_size("gy") - 1
    x_turn = grid_turn(jnp.where(x_last, q_index // (QGRID * QGRID), 0))
    y_turn = grid_turn(jnp.where(y_last, q_index // QGRID % QGRID, 0))
    z_turn = grid_turn(q_index % QGRID)
    real_part, imag_part = rotation_ref[0, 0], rotation_ref[0, 1]
    spread_own = spread_rotation(real_part, imag_part, ROWS)
    spread_ref[...] = spread_rotation(*turned_parts(real_part, imag_part, *x_turn), ROWS)
    edge_mix = spread_rotation(*turned_parts(real_part, imag_part, *y_turn), 1)
    for tile in range(rows // ROWS):
        here = slice(tile * ROWS, (tile + 1) * ROWS)
        for comp in range(COMPS):
            source = jnp.concatenate(
                [
                    u_ref[0, :, comp, :, plane, here, :].reshape(channels * ROWS, lanes)
                    for plane in range(planes)
                ],
                axis=1,
            )
            source = jnp.concatenate([source] * 3, axis=0)
            turned = jnp.dot(spread_own, source, preferred_element_type=F32)
            for plane in range(planes):
                part = turned[:, plane * lanes : (plane + 1) * lanes]
                part = part.reshape(channels, ROWS, lanes)
                modes_ref[plane, comp, :, here, :] = part
                if plane == planes - 1:
                    last_modes_ref[comp, :, here, :] = part
    for plane in range(planes):
        for comp in range(COMPS):
            edge = yrow_ref[comp, plane]
            edge = jnp.concatenate([edge] * 3, axis=0)
            edge = jnp.dot(edge_mix, edge, preferred_element_type=F32)
            modes_ref[plane, comp, :, rows : rows + 1, :] = edge[:, None, :]
        for column in range(3):
            mats_ref[column, plane] = picked(props_ref, column, labels_ref[plane])
            mats_ref[3 + column, plane] = picked(slopes_ref, column, labels_ref[plane])
    lane_at = lax.broadcasted_iota(jnp.int32, (ROWS, lanes), 1)
    is_end = lane_at == lanes - 1
    turn_cos = jnp.where(is_end, z_turn[0], 1.0)
    turn_sin = jnp.where(is_end, z_turn[1], 0.0)

    def per_band(band, carry):
        for plane in range(planes):
            inner = plane < planes - 1
            mass_sum = jnp.zeros((ROWS, lanes), F32)
            stiff_sum = jnp.zeros((ROWS, lanes), F32)
            for tile in range(rows // ROWS):
                begin = tile * ROWS
                here = slice(begin, begin + ROWS)
                after = slice(begin + 1, begin + 1 + ROWS)
                strain_sq = jnp.zeros((ROWS, lanes), F32)
                mass_sq = jnp.zeros((ROWS, lanes), F32)
                dil = [jnp.zeros((ROWS, lanes), F32)] * 2
                for comp in range(COMPS):
                    own = [modes_ref[plane, comp, t * bands + band, here, :] for t in range(2)]
                    roll = [pltpu.roll(v, lanes - 1, 1) for v in own]
                    along_z = [
                        turn_cos * roll[0] - turn_sin * roll[1],
                        turn_sin * roll[0] + turn_cos * roll[1],
                    ]
                    for t in range(2):
                        diff_z = along_z[t] - own[t]
                        diff_y = modes_ref[plane, comp, t * bands + band, after, :] - own[t]
                        strain_sq = strain_sq + diff_z * diff_z + diff_y * diff_y
                        if inner:
                            diff_x = (
                                modes_ref[plane + 1, comp, t * bands + band, here, :] - own[t]
                            )
                            strain_sq = strain_sq + diff_x * diff_x
                            if comp == 0:
                                dil[t] = dil[t] + diff_x
                        if comp == 1:
                            dil[t] = dil[t] + diff_y
                        if comp == 2:
                            dil[t] = dil[t] + diff_z
                        mass_sq = mass_sq + own[t] * own[t]
                mass_sum = mass_sum + mats_ref[2, plane, here, :] * mass_sq
                massd_ref[band, plane, here, :] = mats_ref[5, plane, here, :] * mass_sq
                if inner:
                    dil_sq = dil[0] * dil[0] + dil[1] * dil[1]
                    stiff_sum = (
                        stiff_sum
                        + mats_ref[0, plane, here, :] * strain_sq
                        + mats_ref[1, plane, here, :] * dil_sq
                    )
                    grad_ref[band, plane, here, :] = (
                        mats_ref[3, plane, here, :] * strain_sq
                        + mats_ref[4, plane, here, :] * dil_sq
                    )
                else:
                    strain_ref[band, here, :] = strain_sq
                    dil_ref[0, band, here, :] = dil[0]
                    dil_ref[1, band, here, :] = dil[1]
            acc_ref[plane, band] = stiff_sum
            acc_ref[planes + plane, band] = mass_sum
        return carry

    lax.fori_loop(0, bands, per_band, 0)
    sums_ref[0:bands] = jnp.sum(jnp.sum(acc_ref[0:planes], axis=0), axis=1)
    sums_ref[bands : 2 * bands] = jnp.sum(jnp.sum(acc_ref[planes : 2 * planes], axis=0), axis=1)


def make_edge_kernel(comps, first, last):
    def edge_kernel(mats_ref, spread_ref, modes_ref, strain_ref, dil_ref, sums_in_ref, *refs):
        plane_refs = refs[: len(comps)]
        outs = refs[len(comps) :]
        bands, rows, lanes = strain_ref.shape
        channels = 2 * bands
        next_ref = outs[-1]
        spread = spread_ref[...]
        tiles = rows // ROWS
        for at in range(len(comps)):
            source = jnp.concatenate(
                [
                    plane_refs[at][:, :, tile * ROWS : (tile + 1) * ROWS, :].reshape(
                        channels * ROWS, lanes
                    )
                    for tile in range(tiles)
                ],
                axis=1,
            )
            source = jnp.concatenate([source] * 3, axis=0)
            turned = jnp.dot(spread, source, preferred_element_type=F32)
            for tile in range(tiles):
                next_ref[at, :, tile * ROWS : (tile + 1) * ROWS, :] = turned[
                    :, tile * lanes : (tile + 1) * lanes
                ].reshape(channels, ROWS, lanes)
        last_plane = mats_ref.shape[1] - 1
        for band in range(bands):
            stiff_sum = jnp.zeros((ROWS, lanes), F32)
            for tile in range(tiles):
                here = slice(tile * ROWS, (tile + 1) * ROWS)
                strain_sq = strain_ref[band, here, :]
                dil = []
                for at, comp in enumerate(comps):
                    for t in range(2):
                        diff_x = (
                            next_ref[at, t * bands + band, here, :]
                            - modes_ref[comp, t * bands + band, here, :]
                        )
                        strain_sq = strain_sq + diff_x * diff_x
                        if comp == 0:
                            dil.append(dil_ref[t, band, here, :] + diff_x)
                if dil:
                    dil_sq = dil[0] * dil[0] + dil[1] * dil[1]
                elif last:
                    dil_sq = dil_ref[band, here, :]
                if last:
                    outs[0][band, here, :] = (
                        mats_ref[3, last_plane, here, :] * strain_sq
                        + mats_ref[4, last_plane, here, :] * dil_sq
                    )
                    stiff_sum = (
                        stiff_sum
                        + mats_ref[0, last_plane, here, :] * strain_sq
                        + mats_ref[1, last_plane, here, :] * dil_sq
                    )
                else:
                    outs[0][band, here, :] = strain_sq
                    if dil:
                        outs[1][band, here, :] = dil_sq
            if last:
                outs[1][band : band + 1] = sums_in_ref[band : band + 1] + jnp.sum(
                    stiff_sum, axis=0, keepdims=True
                )
        if last:
            outs[1][bands : 2 * bands] = sums_in_ref[bands : 2 * bands]

    return edge_kernel


def make_combine_kernel(cell_count, slabs):
    def combine_kernel(
        weights_ref, sums_a_ref, sums_b_ref, grad_ref, last_grad_ref, massd_ref, ritz_ref, *slab_refs
    ):
        bands, planes, rows, lanes = massd_ref.shape
        sums = jnp.sum(sums_a_ref[...] + sums_b_ref[...], axis=1, keepdims=True)
        sums = jnp.broadcast_to(sums, (2 * bands, lanes))
        stiff = sums[0:bands]
        inert = sums[bands : 2 * bands]
        ritz = stiff / inert
        band_at = lax.broadcasted_iota(jnp.int32, (bands, lanes), 0)
        weights = jnp.zeros((bands, lanes), F32)
        for band in range(bands):
            weights = jnp.where(band_at == band, weights_ref[0, band], weights)
        factor = weights * (cell_count / inert)
        tail = factor * ritz
        diagonal = band_at == lax.broadcasted_iota(jnp.int32, (bands, lanes), 1)
        ritz_row = jnp.sum(jnp.where(diagonal, ritz, 0.0), axis=0, keepdims=True)
        ritz_ref[...] = ritz_row[:, 0:bands]
        size = rows // slabs
        me = lax.axis_index("ka") if slabs > 1 else 0
        for at in range(slabs):
            begin = pl.multiple_of(lax.rem(me + at, slabs) * size, size) if slabs > 1 else 0
            for plane in range(planes):
                total = jnp.zeros((size, lanes), F32)
                for band in range(bands):
                    if plane < planes - 1:
                        term = grad_ref[band, plane, pl.ds(begin, size), :]
                    else:
                        term = last_grad_ref[band, pl.ds(begin, size), :]
                    total = total + factor[band : band + 1] * term
                    total = total - tail[band : band + 1] * massd_ref[band, plane, pl.ds(begin, size), :]
                slab_refs[at][plane] = total

    return combine_kernel


def on_device(band_fields, labels, phase_props, slopes, kpoints, rotations, band_weights):
    planes, rows, lanes = labels.shape
    bands = band_fields.shape[3]
    channels = 2 * bands
    gx_size = lax.axis_size("gx")
    gy_size = lax.axis_size("gy")
    ka_size = lax.axis_size("ka")
    cell_count = gx_size * gy_size * planes * rows * lanes
    params = pltpu.CompilerParams(vmem_limit_bytes=VMEM_LIMIT)

    sliced = []
    for comp in range(COMPS):
        sliced.append(
            pl.pallas_call(
                make_slice_kernel(comp),
                out_shape=pltpu.VMEM((2, bands, rows, lanes), BF16),
                in_specs=[pl.BlockSpec(memory_space=pl.ANY)] + [vmem] * len(sliced[-1:]),
                out_specs=vmem,
                scratch_shapes=[pltpu.SemaphoreType.DMA(())],
                compiler_params=params,
                name="slice",
            )(band_fields, *[in_vmem(v) for v in sliced[-1:]])
        )
    xplanes = [passed_along(value, "gx", -1) for value in sliced]
    yrow = pl.pallas_call(
        edge_row_kernel,
        out_shape=pltpu.VMEM((COMPS, planes, channels, lanes), BF16),
        in_specs=[
            pl.BlockSpec(
                (1, 2, COMPS, bands, planes, ROWS, lanes), lambda i: (0, 0, 0, 0, 0, 0, 0)
            ),
            vmem,
        ],
        out_specs=pl.BlockSpec((COMPS, planes, channels, lanes), lambda i: (0, 0, 0, 0)),
        grid=(1,),
        compiler_params=params,
        name="edge_row",
    )(band_fields, in_vmem(sliced[-1]))
    yrow = passed_along(yrow, "gy", -1)

    spread, last_modes, grad, massd, strain, dil, sums, mats = pl.pallas_call(
        interior_kernel,
        out_shape=(
            pltpu.VMEM((channels * ROWS, 3 * channels * ROWS), BF16),
            pltpu.VMEM((COMPS, channels, rows, lanes), F32),
            pltpu.VMEM((bands, planes - 1, rows, lanes), F32),
            pltpu.VMEM((bands, planes, rows, lanes), F32),
            pltpu.VMEM((bands, rows, lanes), F32),
            pltpu.VMEM((2, bands, rows, lanes), F32),
            pltpu.VMEM((2 * bands, lanes), F32),
            pltpu.VMEM((6, planes, rows, lanes), F32),
        ),
        in_specs=[smem, smem, smem, vmem, vmem, vmem, vmem],
        out_specs=(vmem,) * 8,
        scratch_shapes=[
            pltpu.VMEM((planes, COMPS, channels, rows + 8, lanes), F32),
            pltpu.VMEM((2 * planes, bands, ROWS, lanes), F32),
        ],
        compiler_params=params,
        name="interior",
    )(kpoints, phase_props, slopes, rotations, labels, band_fields, in_vmem(yrow))

    volume = (bands, rows, lanes)
    for comp in range(COMPS):
        last = comp == COMPS - 1
        if last:
            outs = (pltpu.VMEM(volume, F32), pltpu.VMEM((2 * bands, lanes), F32))
        elif comp == 0:
            outs = (pltpu.VMEM(volume, F32), pltpu.VMEM(volume, F32))
        else:
            outs = (pltpu.VMEM(volume, F32),)
        result = pl.pallas_call(
            make_edge_kernel((comp,), comp == 0, last),
            out_shape=outs,
            in_specs=[vmem] * 7,
            out_specs=(vmem,) * len(outs),
            scratch_shapes=[pltpu.VMEM((1, channels, rows, lanes), F32)],
            compiler_params=params,
            name="edge",
        )(*[in_vmem(v) for v in (mats, spread, last_modes, strain, dil, sums, xplanes[comp])])
        if last:
            last_grad, sums = result
        elif comp == 0:
            strain, dil = result
        else:
            (strain,) = result

    if is_power(gx_size) and is_power(gy_size) and gx_size > 1:
        steps = [("gy", 1 << i) for i in range(gy_size.bit_length() - 1)]
        steps += [("gx", 1 << i) for i in range(gx_size.bit_length() - 1)]
        for axis, flip in steps[:-1]:
            sums = sums + swapped(sums, axis, flip)
        other = swapped(sums, *steps[-1])
    else:
        sums = lax.psum(sums, ("gx", "gy"))
        other = jnp.zeros_like(sums)

    direct = ka_size <= 4 and rows % (8 * ka_size) == 0
    slabs = ka_size if direct else 1
    ritz, *pieces = pl.pallas_call(
        make_combine_kernel(float(cell_count), slabs),
        out_shape=(jax.ShapeDtypeStruct((1, bands), F32),)
        + (pltpu.VMEM((planes, rows // slabs, lanes), F32),) * slabs,
        in_specs=[smem] + [vmem] * 5,
        out_specs=(vmem,) * (1 + slabs),
        compiler_params=params,
        name="combine",
    )(band_weights, *[in_vmem(v) for v in (sums, other, grad, last_grad, massd)])
    if direct:
        design = pieces[0]
        arrived = [passed_along(pieces[hop], "ka", hop) for hop in range(1, slabs)]
        for piece in arrived:
            design = design + piece
    else:
        design = lax.psum_scatter(pieces[0], "ka", scatter_dimension=1, tiled=True)
    return (ritz, design)


def solution(mesh):
    in_specs = (
        P("ka", None, None, None, "gx", "gy", None),
        P("gx", "gy", None),
        P(),
        P(),
        P("ka"),
        P("ka", None, None, None),
        P("ka", None),
    )
    out_specs = (P("ka", None), P("gx", ("gy", "ka"), None))
    return jax.shard_map(
        on_device, mesh=mesh, in_specs=in_specs, out_specs=out_specs, check_vma=False
    )
```

```python
import math

import jax
import jax.numpy as jnp
import numpy as np
from jax import lax
from jax.experimental import pallas as pl
from jax.experimental.pallas import tpu as pltpu
from jax.sharding import PartitionSpec as P

QGRID = 8
PHASES = 3
COMPS = 3
ROWS = 16
F32 = jnp.float32
BF16 = jnp.bfloat16
EXACT = lax.Precision.HIGHEST
VMEM_LIMIT = 56 * 1024 * 1024

vmem = pl.BlockSpec(memory_space=pltpu.VMEM)
smem = pl.BlockSpec(memory_space=pltpu.SMEM)


def in_vmem(value):
    return pltpu.with_memory_space_constraint(value, pltpu.VMEM)


def passed_along(value, axis, by):
    devices = lax.axis_size(axis)
    return lax.ppermute(value, axis, [(i, (i + by) % devices) for i in range(devices)])


def swapped(value, axis, flip):
    devices = lax.axis_size(axis)
    return lax.ppermute(value, axis, [(i, i ^ flip) for i in range(devices)])


def is_power(count):
    return count & (count - 1) == 0


def grid_turn(digit):
    angles = np.arange(QGRID, dtype=np.float32) * np.float32(2.0 * math.pi / QGRID)
    cosine, sine = jnp.float32(1.0), jnp.float32(0.0)
    for at in range(1, QGRID):
        cosine = jnp.where(digit == at, jnp.float32(np.cos(angles[at])), cosine)
        sine = jnp.where(digit == at, jnp.float32(np.sin(angles[at])), sine)
    return cosine, sine


def bf16_parts(value):
    high = value.astype(BF16)
    rest = value - high.astype(F32)
    middle = rest.astype(BF16)
    low = (rest - middle.astype(F32)).astype(BF16)
    return [high, middle, low]


def spread_rotation(real_part, imag_part, rows):
    bands = real_part.shape[0]
    wide = 2 * bands * rows
    tall_at = lax.broadcasted_iota(jnp.int32, (wide, bands), 0) // rows % bands
    tall = (tall_at == lax.broadcasted_iota(jnp.int32, (wide, bands), 1)).astype(F32)
    flat_at = lax.broadcasted_iota(jnp.int32, (bands, wide), 1) // rows % bands
    flat = (flat_at == lax.broadcasted_iota(jnp.int32, (bands, wide), 0)).astype(F32)

    def grown(matrix):
        tall_part = lax.dot_general(
            tall, matrix, (((1,), (1,)), ((), ())), precision=EXACT, preferred_element_type=F32
        )
        return jnp.dot(tall_part, flat, precision=EXACT, preferred_element_type=F32)

    row_at = lax.broadcasted_iota(jnp.int32, (wide, wide), 0)
    column_at = lax.broadcasted_iota(jnp.int32, (wide, wide), 1)
    row_half = row_at // (bands * rows)
    column_half = column_at // (bands * rows)
    real_grown = grown(real_part)
    imag_grown = grown(imag_part)
    imag_grown = jnp.where(row_half > column_half, imag_grown, -imag_grown)
    full = jnp.where(row_half == column_half, real_grown, imag_grown)
    full = jnp.where(row_at % rows == column_at % rows, full, 0.0)
    return jnp.concatenate(bf16_parts(full), axis=1)


def turned_parts(real_part, imag_part, cosine, sine):
    return cosine * real_part - sine * imag_part, sine * real_part + cosine * imag_part


def picked(table, column, label_block):
    low = jnp.where(label_block == 0, table[0, column], table[1, column])
    return jnp.where(label_block == 2, table[2, column], low)


def rows_to_lanes(column, lanes):
    shape = (column.shape[0], lanes)
    diagonal = lax.broadcasted_iota(jnp.int32, shape, 0) == lax.broadcasted_iota(jnp.int32, shape, 1)
    return jnp.sum(jnp.where(diagonal, column, 0.0), axis=0, keepdims=True)


def lanes_to_rows(row, count):
    shape = (count, row.shape[1])
    diagonal = lax.broadcasted_iota(jnp.int32, shape, 0) == lax.broadcasted_iota(jnp.int32, shape, 1)
    return jnp.sum(jnp.where(diagonal, row, 0.0), axis=1, keepdims=True)


def make_slice_kernel(comp):
    def slice_kernel(u_ref, *refs):
        out_ref, sem = refs[-2:]
        copy = pltpu.make_async_copy(u_ref.at[0, :, comp, :, 0], out_ref, sem)
        copy.start()
        copy.wait()

    return slice_kernel


def edge_row_kernel(u_ref, after_ref, out_ref):
    planes = u_ref.shape[4]
    for comp in range(COMPS):
        for plane in range(planes):
            rows = u_ref[0, :, comp, :, plane, 0:1, :]
            out_ref[comp, plane] = rows.reshape(rows.shape[0] * rows.shape[1], rows.shape[3])


def interior_kernel(
    kpoint_ref,
    props_ref,
    slopes_ref,
    weights_in_ref,
    rotation_ref,
    labels_ref,
    u_ref,
    yrow_ref,
    spread_ref,
    last_modes_ref,
    grad_ref,
    massd_ref,
    strain_ref,
    dil_ref,
    sums_ref,
    mats_ref,
    weights_ref,
    modes_ref,
    acc_ref,
):
    planes, rows, lanes = labels_ref.shape
    bands = u_ref.shape[3]
    channels = 2 * bands
    q_index = kpoint_ref[0]
    band_at = lax.broadcasted_iota(jnp.int32, (bands, lanes), 0)
    weights = jnp.zeros((bands, lanes), F32)
    for band in range(bands):
        weights = jnp.where(band_at == band, weights_in_ref[0, band], weights)
    weights_ref[...] = weights
    x_last = lax.axis_index("gx") == lax.axis_size("gx") - 1
    y_last = lax.axis_index("gy") == lax.axis_size("gy") - 1
    x_turn = grid_turn(jnp.where(x_last, q_index // (QGRID * QGRID), 0))
    y_turn = grid_turn(jnp.where(y_last, q_index // QGRID % QGRID, 0))
    z_turn = grid_turn(q_index % QGRID)
    real_part, imag_part = rotation_ref[0, 0], rotation_ref[0, 1]
    spread_own = spread_rotation(real_part, imag_part, ROWS)
    spread_ref[...] = spread_rotation(*turned_parts(real_part, imag_part, *x_turn), ROWS)
    edge_mix = spread_rotation(*turned_parts(real_part, imag_part, *y_turn), 1)
    for tile in range(rows // ROWS):
        here = slice(tile * ROWS, (tile + 1) * ROWS)
        for comp in range(COMPS):
            source = jnp.concatenate(
                [
                    u_ref[0, :, comp, :, plane, here, :].reshape(channels * ROWS, lanes)
                    for plane in range(planes)
                ],
                axis=1,
            )
            source = jnp.concatenate([source] * 3, axis=0)
            turned = jnp.dot(spread_own, source, preferred_element_type=F32)
            for plane in range(planes):
                part = turned[:, plane * lanes : (plane + 1) * lanes]
                part = part.reshape(channels, ROWS, lanes)
                modes_ref[plane, comp, :, here, :] = part
                if plane == planes - 1:
                    last_modes_ref[comp, :, here, :] = part
    for plane in range(planes):
        for comp in range(COMPS):
            edge = yrow_ref[comp, plane]
            edge = jnp.concatenate([edge] * 3, axis=0)
            edge = jnp.dot(edge_mix, edge, preferred_element_type=F32)
            modes_ref[plane, comp, :, rows : rows + 1, :] = edge[:, None, :]
        for column in range(3):
            mats_ref[column, plane] = picked(props_ref, column, labels_ref[plane])
            mats_ref[3 + column, plane] = picked(slopes_ref, column, labels_ref[plane])
    lane_at = lax.broadcasted_iota(jnp.int32, (ROWS, lanes), 1)
    is_end = lane_at == lanes - 1
    turn_cos = jnp.where(is_end, z_turn[0], 1.0)
    turn_sin = jnp.where(is_end, z_turn[1], 0.0)

    def per_band(band, carry):
        for plane in range(planes):
            inner = plane < planes - 1
            mass_sum = jnp.zeros((ROWS, lanes), F32)
            stiff_sum = jnp.zeros((ROWS, lanes), F32)
            for tile in range(rows // ROWS):
                begin = tile * ROWS
                here = slice(begin, begin + ROWS)
                after = slice(begin + 1, begin + 1 + ROWS)
                strain_sq = jnp.zeros((ROWS, lanes), F32)
                mass_sq = jnp.zeros((ROWS, lanes), F32)
                dil = [jnp.zeros((ROWS, lanes), F32)] * 2
                for comp in range(COMPS):
                    own = [modes_ref[plane, comp, t * bands + band, here, :] for t in range(2)]
                    roll = [pltpu.roll(v, lanes - 1, 1) for v in own]
                    along_z = [
                        turn_cos * roll[0] - turn_sin * roll[1],
                        turn_sin * roll[0] + turn_cos * roll[1],
                    ]
                    for t in range(2):
                        diff_z = along_z[t] - own[t]
                        diff_y = modes_ref[plane, comp, t * bands + band, after, :] - own[t]
                        strain_sq = strain_sq + diff_z * diff_z + diff_y * diff_y
                        if inner:
                            diff_x = (
                                modes_ref[plane + 1, comp, t * bands + band, here, :] - own[t]
                            )
                            strain_sq = strain_sq + diff_x * diff_x
                            if comp == 0:
                                dil[t] = dil[t] + diff_x
                        if comp == 1:
                            dil[t] = dil[t] + diff_y
                        if comp == 2:
                            dil[t] = dil[t] + diff_z
                        mass_sq = mass_sq + own[t] * own[t]
                mass_sum = mass_sum + mats_ref[2, plane, here, :] * mass_sq
                massd_ref[band, plane, here, :] = mats_ref[5, plane, here, :] * mass_sq
                if inner:
                    dil_sq = dil[0] * dil[0] + dil[1] * dil[1]
                    stiff_sum = (
                        stiff_sum
                        + mats_ref[0, plane, here, :] * strain_sq
                        + mats_ref[1, plane, here, :] * dil_sq
                    )
                    grad_ref[band, plane, here, :] = (
                        mats_ref[3, plane, here, :] * strain_sq
                        + mats_ref[4, plane, here, :] * dil_sq
                    )
                else:
                    strain_ref[band, here, :] = strain_sq
                    dil_ref[0, band, here, :] = dil[0]
                    dil_ref[1, band, here, :] = dil[1]
            acc_ref[plane, band] = stiff_sum
            acc_ref[planes + plane, band] = mass_sum
        return carry

    lax.fori_loop(0, bands, per_band, 0)
    sums_ref[0:bands] = jnp.sum(jnp.sum(acc_ref[0:planes], axis=0), axis=1)
    sums_ref[bands : 2 * bands] = jnp.sum(jnp.sum(acc_ref[planes : 2 * planes], axis=0), axis=1)


def make_edge_kernel(comps, first, last):
    def edge_kernel(mats_ref, spread_ref, modes_ref, strain_ref, dil_ref, sums_in_ref, *refs):
        plane_refs = refs[: len(comps)]
        outs = refs[len(comps) :]
        bands, rows, lanes = strain_ref.shape
        channels = 2 * bands
        next_ref, acc_ref = outs[-2:]
        spread = spread_ref[...]
        tiles = rows // ROWS
        for at in range(len(comps)):
            source = jnp.concatenate(
                [
                    plane_refs[at][:, :, tile * ROWS : (tile + 1) * ROWS, :].reshape(
                        channels * ROWS, lanes
                    )
                    for tile in range(tiles)
                ],
                axis=1,
            )
            source = jnp.concatenate([source] * 3, axis=0)
            turned = jnp.dot(spread, source, preferred_element_type=F32)
            for tile in range(tiles):
                next_ref[at, :, tile * ROWS : (tile + 1) * ROWS, :] = turned[
                    :, tile * lanes : (tile + 1) * lanes
                ].reshape(channels, ROWS, lanes)
        last_plane = mats_ref.shape[1] - 1
        for band in range(bands):
            stiff_sum = jnp.zeros((ROWS, lanes), F32)
            for tile in range(tiles):
                here = slice(tile * ROWS, (tile + 1) * ROWS)
                strain_sq = strain_ref[band, here, :]
                dil = []
                for at, comp in enumerate(comps):
                    for t in range(2):
                        diff_x = (
                            next_ref[at, t * bands + band, here, :]
                            - modes_ref[comp, t * bands + band, here, :]
                        )
                        strain_sq = strain_sq + diff_x * diff_x
                        if comp == 0:
                            dil.append(dil_ref[t, band, here, :] + diff_x)
                if dil:
                    dil_sq = dil[0] * dil[0] + dil[1] * dil[1]
                elif last:
                    dil_sq = dil_ref[band, here, :]
                if last:
                    outs[0][band, here, :] = (
                        mats_ref[3, last_plane, here, :] * strain_sq
                        + mats_ref[4, last_plane, here, :] * dil_sq
                    )
                    stiff_sum = (
                        stiff_sum
                        + mats_ref[0, last_plane, here, :] * strain_sq
                        + mats_ref[1, last_plane, here, :] * dil_sq
                    )
                else:
                    outs[0][band, here, :] = strain_sq
                    if dil:
                        outs[1][band, here, :] = dil_sq
            if last:
                acc_ref[band : band + 1] = sums_in_ref[band : band + 1] + jnp.sum(
                    stiff_sum, axis=0, keepdims=True
                )
        if last:
            acc_ref[bands : 2 * bands] = sums_in_ref[bands : 2 * bands]
            outs[1][...] = rows_to_lanes(jnp.sum(acc_ref[...], axis=1, keepdims=True), lanes)

    return edge_kernel


def make_combine_kernel(cell_count, slabs):
    def combine_kernel(
        weights_ref, sums_a_ref, sums_b_ref, grad_ref, last_grad_ref, massd_ref, ritz_ref, *slab_refs
    ):
        bands, planes, rows, lanes = massd_ref.shape
        sums = sums_a_ref[...] + sums_b_ref[...]
        sums = jnp.broadcast_to(lanes_to_rows(sums, 2 * bands), (2 * bands, lanes))
        stiff = sums[0:bands]
        inert = sums[bands : 2 * bands]
        ritz = stiff / inert
        factor = weights_ref[...] * (cell_count / inert)
        tail = factor * ritz
        ritz_ref[...] = rows_to_lanes(ritz, lanes)[:, 0:bands]
        size = rows // slabs
        me = lax.axis_index("ka") if slabs > 1 else 0
        for at in range(slabs):
            begin = pl.multiple_of(jnp.bitwise_xor(me, at) * size, size) if slabs > 1 else 0
            for plane in range(planes):
                total = jnp.zeros((size, lanes), F32)
                for band in range(bands):
                    if plane < planes - 1:
                        term = grad_ref[band, plane, pl.ds(begin, size), :]
                    else:
                        term = last_grad_ref[band, pl.ds(begin, size), :]
                    total = total + factor[band : band + 1] * term
                    total = total - tail[band : band + 1] * massd_ref[band, plane, pl.ds(begin, size), :]
                slab_refs[at][plane] = total

    return combine_kernel


def on_device(band_fields, labels, phase_props, slopes, kpoints, rotations, band_weights):
    planes, rows, lanes = labels.shape
    bands = band_fields.shape[3]
    channels = 2 * bands
    gx_size = lax.axis_size("gx")
    gy_size = lax.axis_size("gy")
    ka_size = lax.axis_size("ka")
    cell_count = gx_size * gy_size * planes * rows * lanes
    params = pltpu.CompilerParams(vmem_limit_bytes=VMEM_LIMIT)

    sliced = []
    for comp in range(COMPS):
        sliced.append(
            pl.pallas_call(
                make_slice_kernel(comp),
                out_shape=pltpu.VMEM((2, bands, rows, lanes), BF16),
                in_specs=[pl.BlockSpec(memory_space=pl.ANY)] + [vmem] * len(sliced[-1:]),
                out_specs=vmem,
                scratch_shapes=[pltpu.SemaphoreType.DMA(())],
                compiler_params=params,
                name="slice",
            )(band_fields, *[in_vmem(v) for v in sliced[-1:]])
        )
    xplanes = [passed_along(value, "gx", -1) for value in sliced]
    yrow = pl.pallas_call(
        edge_row_kernel,
        out_shape=pltpu.VMEM((COMPS, planes, channels, lanes), BF16),
        in_specs=[
            pl.BlockSpec(
                (1, 2, COMPS, bands, planes, ROWS, lanes), lambda i: (0, 0, 0, 0, 0, 0, 0)
            ),
            vmem,
        ],
        out_specs=pl.BlockSpec((COMPS, planes, channels, lanes), lambda i: (0, 0, 0, 0)),
        grid=(1,),
        compiler_params=params,
        name="edge_row",
    )(band_fields, in_vmem(sliced[-1]))
    yrow = passed_along(yrow, "gy", -1)

    spread, last_modes, grad, massd, strain, dil, sums, mats, weights = pl.pallas_call(
        interior_kernel,
        out_shape=(
            pltpu.VMEM((channels * ROWS, 3 * channels * ROWS), BF16),
            pltpu.VMEM((COMPS, channels, rows, lanes), F32),
            pltpu.VMEM((bands, planes - 1, rows, lanes), F32),
            pltpu.VMEM((bands, planes, rows, lanes), F32),
            pltpu.VMEM((bands, rows, lanes), F32),
            pltpu.VMEM((2, bands, rows, lanes), F32),
            pltpu.VMEM((2 * bands, lanes), F32),
            pltpu.VMEM((6, planes, rows, lanes), F32),
            pltpu.VMEM((bands, lanes), F32),
        ),
        in_specs=[smem, smem, smem, smem, vmem, vmem, vmem, vmem],
        out_specs=(vmem,) * 9,
        scratch_shapes=[
            pltpu.VMEM((planes, COMPS, channels, rows + 8, lanes), F32),
            pltpu.VMEM((2 * planes, bands, ROWS, lanes), F32),
        ],
        compiler_params=params,
        name="interior",
    )(kpoints, phase_props, slopes, band_weights, rotations, labels, band_fields, in_vmem(yrow))

    volume = (bands, rows, lanes)
    for comp in range(COMPS):
        last = comp == COMPS - 1
        if last:
            outs = (pltpu.VMEM(volume, F32), pltpu.VMEM((1, lanes), F32))
        elif comp == 0:
            outs = (pltpu.VMEM(volume, F32), pltpu.VMEM(volume, F32))
        else:
            outs = (pltpu.VMEM(volume, F32),)
        result = pl.pallas_call(
            make_edge_kernel((comp,), comp == 0, last),
            out_shape=outs,
            in_specs=[vmem] * 7,
            out_specs=(vmem,) * len(outs),
            scratch_shapes=[
                pltpu.VMEM((1, channels, rows, lanes), F32),
                pltpu.VMEM((2 * bands, lanes), F32),
            ],
            compiler_params=params,
            name="edge",
        )(*[in_vmem(v) for v in (mats, spread, last_modes, strain, dil, sums, xplanes[comp])])
        if last:
            last_grad, sums = result
        elif comp == 0:
            strain, dil = result
        else:
            (strain,) = result

    if is_power(gx_size) and is_power(gy_size) and gx_size > 1:
        steps = [("gy", 1 << i) for i in range(gy_size.bit_length() - 1)]
        steps += [("gx", 1 << i) for i in range(gx_size.bit_length() - 1)]
        for axis, flip in steps[:-1]:
            sums = sums + swapped(sums, axis, flip)
        other = swapped(sums, *steps[-1])
    else:
        sums = lax.psum(sums, ("gx", "gy"))
        other = jnp.zeros_like(sums)

    direct = ka_size == 4 and rows % (8 * ka_size) == 0
    slabs = ka_size if direct else 1
    slab = (planes, rows // slabs, lanes)
    slab_shapes = (slab,) * slabs
    ritz, *pieces = pl.pallas_call(
        make_combine_kernel(float(cell_count), slabs),
        out_shape=(pltpu.VMEM((1, bands), F32),)
        + tuple(pltpu.VMEM(shape, F32) for shape in slab_shapes),
        in_specs=[vmem] * 6,
        out_specs=(vmem,) * (1 + len(slab_shapes)),
        compiler_params=params,
        name="combine",
    )(*[in_vmem(v) for v in (weights, sums, other, grad, last_grad, massd)])
    if direct:
        design = pieces[0]
        arrived = [swapped(pieces[hop], "ka", hop) for hop in range(1, slabs)]
        for piece in arrived:
            design = design + piece
    else:
        design = lax.psum_scatter(pieces[0], "ka", scatter_dimension=1, tiled=True)
    return (ritz, design)


def solution(mesh):
    in_specs = (
        P("ka", None, None, None, "gx", "gy", None),
        P("gx", "gy", None),
        P(),
        P(),
        P("ka"),
        P("ka", None, None, None),
        P("ka", None),
    )
    out_specs = (P("ka", None), P("gx", ("gy", "ka"), None))
    return jax.shard_map(
        on_device, mesh=mesh, in_specs=in_specs, out_specs=out_specs, check_vma=False
    )
```

```python
import math

import jax
import jax.numpy as jnp
import numpy as np
from jax import lax
from jax.experimental import pallas as pl
from jax.experimental.pallas import tpu as pltpu
from jax.sharding import PartitionSpec as P

QGRID = 8
PHASES = 3
COMPS = 3
ROWS = 16
F32 = jnp.float32
BF16 = jnp.bfloat16
EXACT = lax.Precision.HIGHEST
VMEM_LIMIT = 56 * 1024 * 1024

vmem = pl.BlockSpec(memory_space=pltpu.VMEM)
smem = pl.BlockSpec(memory_space=pltpu.SMEM)


def in_vmem(value):
    return pltpu.with_memory_space_constraint(value, pltpu.VMEM)


def passed_along(value, axis, by):
    devices = lax.axis_size(axis)
    return lax.ppermute(value, axis, [(i, (i + by) % devices) for i in range(devices)])


def swapped(value, axis, flip):
    devices = lax.axis_size(axis)
    return lax.ppermute(value, axis, [(i, i ^ flip) for i in range(devices)])


def is_power(count):
    return count & (count - 1) == 0


def grid_turn(digit):
    angles = np.arange(QGRID, dtype=np.float32) * np.float32(2.0 * math.pi / QGRID)
    cosine, sine = jnp.float32(1.0), jnp.float32(0.0)
    for at in range(1, QGRID):
        cosine = jnp.where(digit == at, jnp.float32(np.cos(angles[at])), cosine)
        sine = jnp.where(digit == at, jnp.float32(np.sin(angles[at])), sine)
    return cosine, sine


def bf16_parts(value):
    high = value.astype(BF16)
    rest = value - high.astype(F32)
    middle = rest.astype(BF16)
    low = (rest - middle.astype(F32)).astype(BF16)
    return [high, middle, low]


def spread_rotation(real_part, imag_part, rows):
    bands = real_part.shape[0]
    wide = 2 * bands * rows
    tall_at = lax.broadcasted_iota(jnp.int32, (wide, bands), 0) // rows % bands
    tall = (tall_at == lax.broadcasted_iota(jnp.int32, (wide, bands), 1)).astype(F32)
    flat_at = lax.broadcasted_iota(jnp.int32, (bands, wide), 1) // rows % bands
    flat = (flat_at == lax.broadcasted_iota(jnp.int32, (bands, wide), 0)).astype(F32)

    def grown(matrix):
        tall_part = lax.dot_general(
            tall, matrix, (((1,), (1,)), ((), ())), precision=EXACT, preferred_element_type=F32
        )
        return jnp.dot(tall_part, flat, precision=EXACT, preferred_element_type=F32)

    row_at = lax.broadcasted_iota(jnp.int32, (wide, wide), 0)
    column_at = lax.broadcasted_iota(jnp.int32, (wide, wide), 1)
    row_half = row_at // (bands * rows)
    column_half = column_at // (bands * rows)
    real_grown = grown(real_part)
    imag_grown = grown(imag_part)
    imag_grown = jnp.where(row_half > column_half, imag_grown, -imag_grown)
    full = jnp.where(row_half == column_half, real_grown, imag_grown)
    full = jnp.where(row_at % rows == column_at % rows, full, 0.0)
    return jnp.concatenate(bf16_parts(full), axis=1)


def write_spread(out_ref, real_part, imag_part):
    bands = real_part.shape[0]
    half = bands * ROWS
    tall_at = lax.broadcasted_iota(jnp.int32, (half, bands), 0) // ROWS
    tall = (tall_at == lax.broadcasted_iota(jnp.int32, (half, bands), 1)).astype(BF16)
    flat_at = lax.broadcasted_iota(jnp.int32, (bands, half), 1) // ROWS
    flat = (flat_at == lax.broadcasted_iota(jnp.int32, (bands, half), 0)).astype(BF16)
    same_row = (lax.broadcasted_iota(jnp.int32, (half, half), 0) % ROWS) == (
        lax.broadcasted_iota(jnp.int32, (half, half), 1) % ROWS
    )

    def grown(part):
        tall_part = lax.dot_general(
            tall, part, (((1,), (1,)), ((), ())), preferred_element_type=F32
        ).astype(BF16)
        return jnp.where(same_row, jnp.dot(tall_part, flat, preferred_element_type=F32), 0.0)

    parts = zip(bf16_parts(real_part), bf16_parts(imag_part))
    for at, (real_bf16, imag_bf16) in enumerate(parts):
        real_grown, imag_grown = grown(real_bf16), grown(imag_bf16)
        left = slice(2 * at * half, (2 * at + 1) * half)
        right = slice((2 * at + 1) * half, (2 * at + 2) * half)
        out_ref[0:half, left] = real_grown.astype(BF16)
        out_ref[0:half, right] = (-imag_grown).astype(BF16)
        out_ref[half : 2 * half, left] = imag_grown.astype(BF16)
        out_ref[half : 2 * half, right] = real_grown.astype(BF16)


def row_chunks(rows):
    tiles = rows // ROWS
    sizes = [tiles - tiles // 2] + [1] * (tiles // 2)
    chunks, begin = [], 0
    for size in sizes:
        chunks.append((begin, size * ROWS))
        begin += size * ROWS
    return chunks


def turned_parts(real_part, imag_part, cosine, sine):
    return cosine * real_part - sine * imag_part, sine * real_part + cosine * imag_part


def picked(table, column, label_block):
    low = jnp.where(label_block == 0, table[0, column], table[1, column])
    return jnp.where(label_block == 2, table[2, column], low)


def rows_to_lanes(column, lanes):
    shape = (column.shape[0], lanes)
    diagonal = lax.broadcasted_iota(jnp.int32, shape, 0) == lax.broadcasted_iota(jnp.int32, shape, 1)
    return jnp.sum(jnp.where(diagonal, column, 0.0), axis=0, keepdims=True)


def lanes_to_rows(row, count):
    shape = (count, row.shape[1])
    diagonal = lax.broadcasted_iota(jnp.int32, shape, 0) == lax.broadcasted_iota(jnp.int32, shape, 1)
    return jnp.sum(jnp.where(diagonal, row, 0.0), axis=1, keepdims=True)


def make_slice_kernel(begin, size, in_steps):
    def slice_kernel(u_ref, *refs):
        out_ref, sem = refs[-2:]
        source = u_ref.at[0, :, :, :, 0, begin : begin + size]
        whole = pltpu.make_async_copy(source, out_ref, sem)
        if not in_steps:
            whole.start()
            whole.wait()
            return
        second = lax.axis_index("ka") % 2 == 1

        @pl.when(jnp.logical_not(second))
        def _():
            whole.start()
            whole.wait()

        @pl.when(second)
        def _():
            for t in range(2):
                for comp in range(COMPS):
                    piece = pltpu.make_async_copy(source.at[t, comp], out_ref.at[t, comp], sem)
                    piece.start()
                    piece.wait()

    return slice_kernel


def edge_row_kernel(u_ref, after_ref, out_ref):
    planes = u_ref.shape[4]
    for comp in range(COMPS):
        for plane in range(planes):
            rows = u_ref[0, :, comp, :, plane, 0:1, :]
            out_ref[comp, plane] = rows.reshape(rows.shape[0] * rows.shape[1], rows.shape[3])


def interior_kernel(
    kpoint_ref,
    props_ref,
    slopes_ref,
    weights_in_ref,
    rotation_ref,
    labels_ref,
    u_ref,
    yrow_ref,
    spread_ref,
    last_modes_ref,
    grad_ref,
    massd_ref,
    strain_ref,
    dil_ref,
    sums_ref,
    mats_ref,
    weights_ref,
    modes_ref,
    acc_ref,
    own_ref,
):
    planes, rows, lanes = labels_ref.shape
    bands = u_ref.shape[3]
    channels = 2 * bands
    q_index = kpoint_ref[0, 0]
    band_at = lax.broadcasted_iota(jnp.int32, (bands, lanes), 0)
    weights = jnp.zeros((bands, lanes), F32)
    for band in range(bands):
        weights = jnp.where(band_at == band, weights_in_ref[0, band], weights)
    weights_ref[...] = weights
    x_last = lax.axis_index("gx") == lax.axis_size("gx") - 1
    y_last = lax.axis_index("gy") == lax.axis_size("gy") - 1
    x_turn = grid_turn(jnp.where(x_last, q_index // (QGRID * QGRID), 0))
    y_turn = grid_turn(jnp.where(y_last, q_index // QGRID % QGRID, 0))
    z_turn = grid_turn(q_index % QGRID)
    real_part, imag_part = rotation_ref[0, 0], rotation_ref[0, 1]
    write_spread(own_ref, real_part, imag_part)
    write_spread(spread_ref, *turned_parts(real_part, imag_part, *x_turn))
    spread_own = own_ref[...]
    edge_mix = spread_rotation(*turned_parts(real_part, imag_part, *y_turn), 1)
    for tile in range(rows // ROWS):
        here = slice(tile * ROWS, (tile + 1) * ROWS)
        for comp in range(COMPS):
            source = jnp.concatenate(
                [
                    u_ref[0, :, comp, :, plane, here, :].reshape(channels * ROWS, lanes)
                    for plane in range(planes)
                ],
                axis=1,
            )
            source = jnp.concatenate([source] * 3, axis=0)
            turned = jnp.dot(spread_own, source, preferred_element_type=F32)
            for plane in range(planes):
                part = turned[:, plane * lanes : (plane + 1) * lanes]
                part = part.reshape(channels, ROWS, lanes)
                modes_ref[plane, comp, :, here, :] = part
                if plane == planes - 1:
                    last_modes_ref[comp, :, here, :] = part
    for plane in range(planes):
        for comp in range(COMPS):
            edge = yrow_ref[comp, plane]
            edge = jnp.concatenate([edge] * 3, axis=0)
            edge = jnp.dot(edge_mix, edge, preferred_element_type=F32)
            modes_ref[plane, comp, :, rows : rows + 1, :] = edge[:, None, :]
        for column in range(3):
            mats_ref[column, plane] = picked(props_ref, column, labels_ref[plane])
            mats_ref[3 + column, plane] = picked(slopes_ref, column, labels_ref[plane])
    lane_at = lax.broadcasted_iota(jnp.int32, (ROWS, lanes), 1)
    is_end = lane_at == lanes - 1
    turn_cos = jnp.where(is_end, z_turn[0], 1.0)
    turn_sin = jnp.where(is_end, z_turn[1], 0.0)

    def per_band(band, carry):
        for plane in range(planes):
            inner = plane < planes - 1
            mass_sum = jnp.zeros((ROWS, lanes), F32)
            stiff_sum = jnp.zeros((ROWS, lanes), F32)
            for tile in range(rows // ROWS):
                begin = tile * ROWS
                here = slice(begin, begin + ROWS)
                after = slice(begin + 1, begin + 1 + ROWS)
                strain_sq = jnp.zeros((ROWS, lanes), F32)
                mass_sq = jnp.zeros((ROWS, lanes), F32)
                dil = [jnp.zeros((ROWS, lanes), F32)] * 2
                for comp in range(COMPS):
                    own = [modes_ref[plane, comp, t * bands + band, here, :] for t in range(2)]
                    roll = [pltpu.roll(v, lanes - 1, 1) for v in own]
                    along_z = [
                        turn_cos * roll[0] - turn_sin * roll[1],
                        turn_sin * roll[0] + turn_cos * roll[1],
                    ]
                    for t in range(2):
                        diff_z = along_z[t] - own[t]
                        diff_y = modes_ref[plane, comp, t * bands + band, after, :] - own[t]
                        strain_sq = strain_sq + diff_z * diff_z + diff_y * diff_y
                        if inner:
                            diff_x = (
                                modes_ref[plane + 1, comp, t * bands + band, here, :] - own[t]
                            )
                            strain_sq = strain_sq + diff_x * diff_x
                            if comp == 0:
                                dil[t] = dil[t] + diff_x
                        if comp == 1:
                            dil[t] = dil[t] + diff_y
                        if comp == 2:
                            dil[t] = dil[t] + diff_z
                        mass_sq = mass_sq + own[t] * own[t]
                mass_sum = mass_sum + mats_ref[2, plane, here, :] * mass_sq
                massd_ref[band, plane, here, :] = mats_ref[5, plane, here, :] * mass_sq
                if inner:
                    dil_sq = dil[0] * dil[0] + dil[1] * dil[1]
                    stiff_sum = (
                        stiff_sum
                        + mats_ref[0, plane, here, :] * strain_sq
                        + mats_ref[1, plane, here, :] * dil_sq
                    )
                    grad_ref[band, plane, here, :] = (
                        mats_ref[3, plane, here, :] * strain_sq
                        + mats_ref[4, plane, here, :] * dil_sq
                    )
                else:
                    strain_ref[band, here, :] = strain_sq
                    dil_ref[0, band, here, :] = dil[0]
                    dil_ref[1, band, here, :] = dil[1]
            acc_ref[plane, band] = stiff_sum
            acc_ref[planes + plane, band] = mass_sum
        return carry

    lax.fori_loop(0, bands, per_band, 0)
    sums_ref[0:bands] = jnp.sum(jnp.sum(acc_ref[0:planes], axis=0), axis=1)
    sums_ref[bands : 2 * bands] = jnp.sum(jnp.sum(acc_ref[planes : 2 * planes], axis=0), axis=1)


def make_edge_kernel(begin, size, last):
    def edge_kernel(
        mats_ref,
        spread_ref,
        modes_ref,
        strain_ref,
        dil_ref,
        sums_in_ref,
        plane_ref,
        grad_ref,
        sums_ref,
        next_ref,
        acc_ref,
    ):
        bands, _, lanes = strain_ref.shape
        channels = 2 * bands
        tiles = size // ROWS
        blocks = [(comp, tile) for comp in range(COMPS) for tile in range(tiles)]
        source = jnp.concatenate(
            [
                plane_ref[:, comp, :, tile * ROWS : (tile + 1) * ROWS, :].reshape(
                    channels * ROWS, lanes
                )
                for comp, tile in blocks
            ],
            axis=1,
        )
        source = jnp.concatenate([source] * 3, axis=0)
        turned = jnp.dot(spread_ref[...], source, preferred_element_type=F32)
        for at, (comp, tile) in enumerate(blocks):
            next_ref[comp, :, tile * ROWS : (tile + 1) * ROWS, :] = turned[
                :, at * lanes : (at + 1) * lanes
            ].reshape(channels, ROWS, lanes)
        plane = mats_ref.shape[1] - 1
        for band in range(bands):
            stiff_sum = jnp.zeros((ROWS, lanes), F32)
            for tile in range(tiles):
                here = slice(begin + tile * ROWS, begin + (tile + 1) * ROWS)
                there = slice(tile * ROWS, (tile + 1) * ROWS)
                strain_sq = strain_ref[band, here, :]
                dil = [dil_ref[t, band, here, :] for t in range(2)]
                for comp in range(COMPS):
                    for t in range(2):
                        diff_x = (
                            next_ref[comp, t * bands + band, there, :]
                            - modes_ref[comp, t * bands + band, here, :]
                        )
                        strain_sq = strain_sq + diff_x * diff_x
                        if comp == 0:
                            dil[t] = dil[t] + diff_x
                dil_sq = dil[0] * dil[0] + dil[1] * dil[1]
                grad_ref[band, there, :] = (
                    mats_ref[3, plane, here, :] * strain_sq + mats_ref[4, plane, here, :] * dil_sq
                )
                stiff_sum = (
                    stiff_sum
                    + mats_ref[0, plane, here, :] * strain_sq
                    + mats_ref[1, plane, here, :] * dil_sq
                )
            acc_ref[band : band + 1] = sums_in_ref[band : band + 1] + jnp.sum(
                stiff_sum, axis=0, keepdims=True
            )
        acc_ref[bands : 2 * bands] = sums_in_ref[bands : 2 * bands]
        if last:
            sums_ref[...] = rows_to_lanes(jnp.sum(acc_ref[...], axis=1, keepdims=True), lanes)
        else:
            sums_ref[...] = acc_ref[...]

    return edge_kernel


def make_combine_kernel(cell_count, slabs, chunks):
    def combine_kernel(weights_ref, sums_a_ref, sums_b_ref, grad_ref, massd_ref, *refs):
        last_grad_refs = refs[: len(chunks)]
        ritz_ref, slab_refs = refs[len(chunks)], refs[len(chunks) + 1 :]
        bands, planes, rows, lanes = massd_ref.shape
        sums = sums_a_ref[...] + sums_b_ref[...]
        sums = jnp.broadcast_to(lanes_to_rows(sums, 2 * bands), (2 * bands, lanes))
        stiff = sums[0:bands]
        inert = sums[bands : 2 * bands]
        ritz = stiff / inert
        factor = weights_ref[...] * (cell_count / inert)
        tail = factor * ritz
        ritz_ref[...] = rows_to_lanes(ritz, lanes)[:, 0:bands]
        tiles = rows // ROWS // slabs
        me = lax.axis_index("ka") if slabs > 1 else 0
        for plane in range(planes):
            totals = []
            for begin in range(0, rows, ROWS):
                here = slice(begin, begin + ROWS)
                part = [i for i, (first, size) in enumerate(chunks) if first <= begin < first + size][0]
                there = slice(begin - chunks[part][0], begin - chunks[part][0] + ROWS)
                total = jnp.zeros((ROWS, lanes), F32)
                for band in range(bands):
                    if plane < planes - 1:
                        term = grad_ref[band, plane, here, :]
                    else:
                        term = last_grad_refs[part][band, there, :]
                    total = total + factor[band : band + 1] * term
                    total = total - tail[band : band + 1] * massd_ref[band, plane, here, :]
                totals.append(total)
            for at in range(slabs):
                for tile in range(tiles):
                    value = totals[at * tiles + tile]
                    for other in range(1, slabs):
                        value = jnp.where(me == other, totals[(at ^ other) * tiles + tile], value)
                    slab_refs[at][plane, tile * ROWS : (tile + 1) * ROWS, :] = value

    return combine_kernel


def on_device(band_fields, labels, phase_props, slopes, kpoints, rotations, band_weights):
    planes, rows, lanes = labels.shape
    bands = band_fields.shape[3]
    channels = 2 * bands
    gx_size = lax.axis_size("gx")
    gy_size = lax.axis_size("gy")
    ka_size = lax.axis_size("ka")
    cell_count = gx_size * gy_size * planes * rows * lanes
    params = pltpu.CompilerParams(vmem_limit_bytes=VMEM_LIMIT)

    chunks = row_chunks(rows)
    sliced, yrow = [], None
    for begin, size in chunks:
        behind = sliced[-1:] if yrow is None or len(sliced) > 1 else [yrow]
        sliced.append(
            pl.pallas_call(
                make_slice_kernel(begin, size, not sliced),
                out_shape=pltpu.VMEM((2, COMPS, bands, size, lanes), BF16),
                in_specs=[pl.BlockSpec(memory_space=pl.ANY)] + [vmem] * len(behind),
                out_specs=vmem,
                scratch_shapes=[pltpu.SemaphoreType.DMA(())],
                compiler_params=params,
                name="slice",
            )(band_fields, *[in_vmem(v) for v in behind])
        )
        if yrow is None:
            yrow = pl.pallas_call(
                edge_row_kernel,
                out_shape=pltpu.VMEM((COMPS, planes, channels, lanes), BF16),
                in_specs=[
                    pl.BlockSpec(
                        (1, 2, COMPS, bands, planes, ROWS, lanes), lambda i: (0, 0, 0, 0, 0, 0, 0)
                    ),
                    vmem,
                ],
                out_specs=pl.BlockSpec((COMPS, planes, channels, lanes), lambda i: (0, 0, 0, 0)),
                grid=(1,),
                compiler_params=params,
                name="edge_row",
            )(band_fields, in_vmem(sliced[0]))
    xplanes = [passed_along(value, "gx", -1) for value in sliced]
    yrow = passed_along(yrow, "gy", -1)

    spread, last_modes, grad, massd, strain, dil, sums, mats, weights = pl.pallas_call(
        interior_kernel,
        out_shape=(
            pltpu.VMEM((channels * ROWS, 3 * channels * ROWS), BF16),
            pltpu.VMEM((COMPS, channels, rows, lanes), F32),
            pltpu.VMEM((bands, planes - 1, rows, lanes), F32),
            pltpu.VMEM((bands, planes, rows, lanes), F32),
            pltpu.VMEM((bands, rows, lanes), F32),
            pltpu.VMEM((2, bands, rows, lanes), F32),
            pltpu.VMEM((2 * bands, lanes), F32),
            pltpu.VMEM((6, planes, rows, lanes), F32),
            pltpu.VMEM((bands, lanes), F32),
        ),
        in_specs=[smem, smem, smem, smem, vmem, vmem, vmem, vmem],
        out_specs=(vmem,) * 9,
        scratch_shapes=[
            pltpu.VMEM((planes, COMPS, channels, rows + 8, lanes), F32),
            pltpu.VMEM((2 * planes, bands, ROWS, lanes), F32),
            pltpu.VMEM((channels * ROWS, 3 * channels * ROWS), BF16),
        ],
        compiler_params=params,
        name="interior",
    )(kpoints.reshape(1, 1), phase_props, slopes, band_weights, rotations, labels, band_fields, in_vmem(yrow))

    last_grads = []
    for (begin, size), xplane in zip(chunks, xplanes):
        last = len(last_grads) == len(chunks) - 1
        last_grad, sums = pl.pallas_call(
            make_edge_kernel(begin, size, last),
            out_shape=(
                pltpu.VMEM((bands, size, lanes), F32),
                pltpu.VMEM((1 if last else 2 * bands, lanes), F32),
            ),
            in_specs=[vmem] * 7,
            out_specs=(vmem, vmem),
            scratch_shapes=[
                pltpu.VMEM((COMPS, channels, size, lanes), F32),
                pltpu.VMEM((2 * bands, lanes), F32),
            ],
            compiler_params=params,
            name="edge",
        )(*[in_vmem(v) for v in (mats, spread, last_modes, strain, dil, sums, xplane)])
        last_grads.append(last_grad)

    if is_power(gx_size) and is_power(gy_size) and gx_size > 1:
        steps = [("gy", 1 << i) for i in range(gy_size.bit_length() - 1)]
        steps += [("gx", 1 << i) for i in range(gx_size.bit_length() - 1)]
        for axis, flip in steps[:-1]:
            sums = sums + swapped(sums, axis, flip)
        other = swapped(sums, *steps[-1])
    else:
        sums = lax.psum(sums, ("gx", "gy"))
        other = jnp.zeros_like(sums)

    direct = ka_size == 4 and rows % (ROWS * ka_size) == 0
    slabs = ka_size if direct else 1
    slab = (planes, rows // slabs, lanes)
    slab_shapes = (slab,) * slabs
    ritz, *pieces = pl.pallas_call(
        make_combine_kernel(float(cell_count), slabs, chunks),
        out_shape=(pltpu.VMEM((1, bands), F32),)
        + tuple(pltpu.VMEM(shape, F32) for shape in slab_shapes),
        in_specs=[vmem] * (5 + len(chunks)),
        out_specs=(vmem,) * (1 + len(slab_shapes)),
        compiler_params=params,
        name="combine",
    )(*[in_vmem(v) for v in (weights, sums, other, grad, massd, *last_grads)])
    if direct:
        design = pieces[0]
        arrived = [swapped(pieces[hop], "ka", hop) for hop in range(1, slabs)]
        for piece in arrived:
            design = design + piece
    else:
        design = lax.psum_scatter(pieces[0], "ka", scatter_dimension=1, tiled=True)
    return (ritz, design)


def solution(mesh):
    in_specs = (
        P("ka", None, None, None, "gx", "gy", None),
        P("gx", "gy", None),
        P(),
        P(),
        P("ka"),
        P("ka", None, None, None),
        P("ka", None),
    )
    out_specs = (P("ka", None), P("gx", ("gy", "ka"), None))
    return jax.shard_map(
        on_device, mesh=mesh, in_specs=in_specs, out_specs=out_specs, check_vma=False
    )
```

```python
import math

import jax
import jax.numpy as jnp
import numpy as np
from jax import lax
from jax.experimental import pallas as pl
from jax.experimental.pallas import tpu as pltpu
from jax.sharding import PartitionSpec as P

QGRID = 8
PHASES = 3
COMPS = 3
ROWS = 16
F32 = jnp.float32
BF16 = jnp.bfloat16
EXACT = lax.Precision.HIGHEST
VMEM_LIMIT = 56 * 1024 * 1024

vmem = pl.BlockSpec(memory_space=pltpu.VMEM)
smem = pl.BlockSpec(memory_space=pltpu.SMEM)


def in_vmem(value):
    return pltpu.with_memory_space_constraint(value, pltpu.VMEM)


def passed_along(value, axis, by):
    devices = lax.axis_size(axis)
    return lax.ppermute(value, axis, [(i, (i + by) % devices) for i in range(devices)])


def swapped(value, axis, flip):
    devices = lax.axis_size(axis)
    return lax.ppermute(value, axis, [(i, i ^ flip) for i in range(devices)])


def is_power(count):
    return count & (count - 1) == 0


def grid_turn(digit):
    angles = np.arange(QGRID, dtype=np.float32) * np.float32(2.0 * math.pi / QGRID)
    cosine, sine = jnp.float32(1.0), jnp.float32(0.0)
    for at in range(1, QGRID):
        cosine = jnp.where(digit == at, jnp.float32(np.cos(angles[at])), cosine)
        sine = jnp.where(digit == at, jnp.float32(np.sin(angles[at])), sine)
    return cosine, sine


def bf16_parts(value):
    high = value.astype(BF16)
    rest = value - high.astype(F32)
    middle = rest.astype(BF16)
    low = (rest - middle.astype(F32)).astype(BF16)
    return [high, middle, low]


def spread_rotation(real_part, imag_part, rows):
    bands = real_part.shape[0]
    wide = 2 * bands * rows
    tall_at = lax.broadcasted_iota(jnp.int32, (wide, bands), 0) // rows % bands
    tall = (tall_at == lax.broadcasted_iota(jnp.int32, (wide, bands), 1)).astype(F32)
    flat_at = lax.broadcasted_iota(jnp.int32, (bands, wide), 1) // rows % bands
    flat = (flat_at == lax.broadcasted_iota(jnp.int32, (bands, wide), 0)).astype(F32)

    def grown(matrix):
        tall_part = lax.dot_general(
            tall, matrix, (((1,), (1,)), ((), ())), precision=EXACT, preferred_element_type=F32
        )
        return jnp.dot(tall_part, flat, precision=EXACT, preferred_element_type=F32)

    row_at = lax.broadcasted_iota(jnp.int32, (wide, wide), 0)
    column_at = lax.broadcasted_iota(jnp.int32, (wide, wide), 1)
    row_half = row_at // (bands * rows)
    column_half = column_at // (bands * rows)
    real_grown = grown(real_part)
    imag_grown = grown(imag_part)
    imag_grown = jnp.where(row_half > column_half, imag_grown, -imag_grown)
    full = jnp.where(row_half == column_half, real_grown, imag_grown)
    full = jnp.where(row_at % rows == column_at % rows, full, 0.0)
    return jnp.concatenate(bf16_parts(full), axis=1)


def write_spread(out_ref, real_part, imag_part):
    bands = real_part.shape[0]
    half = bands * ROWS
    tall_at = lax.broadcasted_iota(jnp.int32, (half, bands), 0) // ROWS
    tall = (tall_at == lax.broadcasted_iota(jnp.int32, (half, bands), 1)).astype(BF16)
    flat_at = lax.broadcasted_iota(jnp.int32, (bands, half), 1) // ROWS
    flat = (flat_at == lax.broadcasted_iota(jnp.int32, (bands, half), 0)).astype(BF16)
    same_row = (lax.broadcasted_iota(jnp.int32, (half, half), 0) % ROWS) == (
        lax.broadcasted_iota(jnp.int32, (half, half), 1) % ROWS
    )

    def grown(part):
        tall_part = lax.dot_general(
            tall, part, (((1,), (1,)), ((), ())), preferred_element_type=F32
        ).astype(BF16)
        return jnp.where(same_row, jnp.dot(tall_part, flat, preferred_element_type=F32), 0.0)

    parts = zip(bf16_parts(real_part), bf16_parts(imag_part))
    for at, (real_bf16, imag_bf16) in enumerate(parts):
        real_grown, imag_grown = grown(real_bf16), grown(imag_bf16)
        left = slice(2 * at * half, (2 * at + 1) * half)
        right = slice((2 * at + 1) * half, (2 * at + 2) * half)
        out_ref[0:half, left] = real_grown.astype(BF16)
        out_ref[0:half, right] = (-imag_grown).astype(BF16)
        out_ref[half : 2 * half, left] = imag_grown.astype(BF16)
        out_ref[half : 2 * half, right] = real_grown.astype(BF16)


def row_chunks(rows):
    tiles = rows // ROWS
    sizes = [tiles - tiles // 2] + [1] * (tiles // 2)
    chunks, begin = [], 0
    for size in sizes:
        chunks.append((begin, size * ROWS))
        begin += size * ROWS
    return chunks


def turned_parts(real_part, imag_part, cosine, sine):
    return cosine * real_part - sine * imag_part, sine * real_part + cosine * imag_part


def picked(table, column, label_block):
    low = jnp.where(label_block == 0, table[0, column], table[1, column])
    return jnp.where(label_block == 2, table[2, column], low)


def rows_to_lanes(column, lanes):
    shape = (column.shape[0], lanes)
    diagonal = lax.broadcasted_iota(jnp.int32, shape, 0) == lax.broadcasted_iota(jnp.int32, shape, 1)
    return jnp.sum(jnp.where(diagonal, column, 0.0), axis=0, keepdims=True)


def lanes_to_rows(row, count):
    shape = (count, row.shape[1])
    diagonal = lax.broadcasted_iota(jnp.int32, shape, 0) == lax.broadcasted_iota(jnp.int32, shape, 1)
    return jnp.sum(jnp.where(diagonal, row, 0.0), axis=1, keepdims=True)


def make_slice_kernel(begin, size, in_steps):
    def slice_kernel(u_ref, *refs):
        out_ref, sem = refs[-2:]
        source = u_ref.at[0, :, :, :, 0, begin : begin + size]
        whole = pltpu.make_async_copy(source, out_ref, sem)
        if not in_steps:
            whole.start()
            whole.wait()
            return
        second = lax.axis_index("ka") % 2 == 1

        @pl.when(jnp.logical_not(second))
        def _():
            whole.start()
            whole.wait()

        @pl.when(second)
        def _():
            for band in range(out_ref.shape[2]):
                piece = pltpu.make_async_copy(source.at[:, :, band], out_ref.at[:, :, band], sem)
                piece.start()
                piece.wait()

    return slice_kernel


def edge_row_kernel(u_ref, after_ref, out_ref):
    planes = u_ref.shape[4]
    for comp in range(COMPS):
        for plane in range(planes):
            rows = u_ref[0, :, comp, :, plane, 0:1, :]
            out_ref[comp, plane] = rows.reshape(rows.shape[0] * rows.shape[1], rows.shape[3])


def interior_kernel(
    kpoint_ref,
    props_ref,
    slopes_ref,
    weights_in_ref,
    rotation_ref,
    labels_ref,
    u_ref,
    yrow_ref,
    spread_ref,
    last_modes_ref,
    grad_ref,
    massd_ref,
    strain_ref,
    dil_ref,
    sums_ref,
    mats_ref,
    weights_ref,
    modes_ref,
    acc_ref,
    own_ref,
):
    planes, rows, lanes = labels_ref.shape
    bands = u_ref.shape[3]
    channels = 2 * bands
    q_index = kpoint_ref[0, 0]
    band_at = lax.broadcasted_iota(jnp.int32, (bands, lanes), 0)
    weights = jnp.zeros((bands, lanes), F32)
    for band in range(bands):
        weights = jnp.where(band_at == band, weights_in_ref[0, band], weights)
    weights_ref[...] = weights
    x_last = lax.axis_index("gx") == lax.axis_size("gx") - 1
    y_last = lax.axis_index("gy") == lax.axis_size("gy") - 1
    x_turn = grid_turn(jnp.where(x_last, q_index // (QGRID * QGRID), 0))
    y_turn = grid_turn(jnp.where(y_last, q_index // QGRID % QGRID, 0))
    z_turn = grid_turn(q_index % QGRID)
    real_part, imag_part = rotation_ref[0, 0], rotation_ref[0, 1]
    write_spread(own_ref, real_part, imag_part)
    write_spread(spread_ref, *turned_parts(real_part, imag_part, *x_turn))
    spread_own = own_ref[...]
    edge_mix = spread_rotation(*turned_parts(real_part, imag_part, *y_turn), 1)
    for tile in range(rows // ROWS):
        here = slice(tile * ROWS, (tile + 1) * ROWS)
        for comp in range(COMPS):
            source = jnp.concatenate(
                [
                    u_ref[0, :, comp, :, plane, here, :].reshape(channels * ROWS, lanes)
                    for plane in range(planes)
                ],
                axis=1,
            )
            source = jnp.concatenate([source] * 3, axis=0)
            turned = jnp.dot(spread_own, source, preferred_element_type=F32)
            for plane in range(planes):
                part = turned[:, plane * lanes : (plane + 1) * lanes]
                part = part.reshape(channels, ROWS, lanes)
                modes_ref[plane, comp, :, here, :] = part
                if plane == planes - 1:
                    last_modes_ref[comp, :, here, :] = part
    for plane in range(planes):
        for comp in range(COMPS):
            edge = yrow_ref[comp, plane]
            edge = jnp.concatenate([edge] * 3, axis=0)
            edge = jnp.dot(edge_mix, edge, preferred_element_type=F32)
            modes_ref[plane, comp, :, rows : rows + 1, :] = edge[:, None, :]
        for column in range(3):
            mats_ref[column, plane] = picked(props_ref, column, labels_ref[plane])
            mats_ref[3 + column, plane] = picked(slopes_ref, column, labels_ref[plane])
    lane_at = lax.broadcasted_iota(jnp.int32, (ROWS, lanes), 1)
    is_end = lane_at == lanes - 1
    turn_cos = jnp.where(is_end, z_turn[0], 1.0)
    turn_sin = jnp.where(is_end, z_turn[1], 0.0)

    def per_band(band, carry):
        for plane in range(planes):
            inner = plane < planes - 1
            mass_sum = jnp.zeros((ROWS, lanes), F32)
            stiff_sum = jnp.zeros((ROWS, lanes), F32)
            for tile in range(rows // ROWS):
                begin = tile * ROWS
                here = slice(begin, begin + ROWS)
                after = slice(begin + 1, begin + 1 + ROWS)
                strain_sq = jnp.zeros((ROWS, lanes), F32)
                mass_sq = jnp.zeros((ROWS, lanes), F32)
                dil = [jnp.zeros((ROWS, lanes), F32)] * 2
                for comp in range(COMPS):
                    own = [modes_ref[plane, comp, t * bands + band, here, :] for t in range(2)]
                    roll = [pltpu.roll(v, lanes - 1, 1) for v in own]
                    along_z = [
                        turn_cos * roll[0] - turn_sin * roll[1],
                        turn_sin * roll[0] + turn_cos * roll[1],
                    ]
                    for t in range(2):
                        diff_z = along_z[t] - own[t]
                        diff_y = modes_ref[plane, comp, t * bands + band, after, :] - own[t]
                        strain_sq = strain_sq + diff_z * diff_z + diff_y * diff_y
                        if inner:
                            diff_x = (
                                modes_ref[plane + 1, comp, t * bands + band, here, :] - own[t]
                            )
                            strain_sq = strain_sq + diff_x * diff_x
                            if comp == 0:
                                dil[t] = dil[t] + diff_x
                        if comp == 1:
                            dil[t] = dil[t] + diff_y
                        if comp == 2:
                            dil[t] = dil[t] + diff_z
                        mass_sq = mass_sq + own[t] * own[t]
                mass_sum = mass_sum + mats_ref[2, plane, here, :] * mass_sq
                massd_ref[band, plane, here, :] = mats_ref[5, plane, here, :] * mass_sq
                if inner:
                    dil_sq = dil[0] * dil[0] + dil[1] * dil[1]
                    stiff_sum = (
                        stiff_sum
                        + mats_ref[0, plane, here, :] * strain_sq
                        + mats_ref[1, plane, here, :] * dil_sq
                    )
                    grad_ref[band, plane, here, :] = (
                        mats_ref[3, plane, here, :] * strain_sq
                        + mats_ref[4, plane, here, :] * dil_sq
                    )
                else:
                    strain_ref[band, here, :] = strain_sq
                    dil_ref[0, band, here, :] = dil[0]
                    dil_ref[1, band, here, :] = dil[1]
            acc_ref[plane, band] = stiff_sum
            acc_ref[planes + plane, band] = mass_sum
        return carry

    lax.fori_loop(0, bands, per_band, 0)
    sums_ref[0:bands] = jnp.sum(jnp.sum(acc_ref[0:planes], axis=0), axis=1)
    sums_ref[bands : 2 * bands] = jnp.sum(jnp.sum(acc_ref[planes : 2 * planes], axis=0), axis=1)


def make_edge_kernel(begin, size, last):
    def edge_kernel(
        mats_ref,
        spread_ref,
        modes_ref,
        strain_ref,
        dil_ref,
        sums_in_ref,
        plane_ref,
        grad_ref,
        sums_ref,
        next_ref,
        acc_ref,
    ):
        bands, _, lanes = strain_ref.shape
        channels = 2 * bands
        tiles = size // ROWS
        blocks = [(comp, tile) for comp in range(COMPS) for tile in range(tiles)]
        source = jnp.concatenate(
            [
                plane_ref[:, comp, :, tile * ROWS : (tile + 1) * ROWS, :].reshape(
                    channels * ROWS, lanes
                )
                for comp, tile in blocks
            ],
            axis=1,
        )
        source = jnp.concatenate([source] * 3, axis=0)
        turned = jnp.dot(spread_ref[...], source, preferred_element_type=F32)
        for at, (comp, tile) in enumerate(blocks):
            next_ref[comp, :, tile * ROWS : (tile + 1) * ROWS, :] = turned[
                :, at * lanes : (at + 1) * lanes
            ].reshape(channels, ROWS, lanes)
        plane = mats_ref.shape[1] - 1
        for band in range(bands):
            stiff_sum = jnp.zeros((ROWS, lanes), F32)
            for tile in range(tiles):
                here = slice(begin + tile * ROWS, begin + (tile + 1) * ROWS)
                there = slice(tile * ROWS, (tile + 1) * ROWS)
                strain_sq = strain_ref[band, here, :]
                dil = [dil_ref[t, band, here, :] for t in range(2)]
                for comp in range(COMPS):
                    for t in range(2):
                        diff_x = (
                            next_ref[comp, t * bands + band, there, :]
                            - modes_ref[comp, t * bands + band, here, :]
                        )
                        strain_sq = strain_sq + diff_x * diff_x
                        if comp == 0:
                            dil[t] = dil[t] + diff_x
                dil_sq = dil[0] * dil[0] + dil[1] * dil[1]
                grad_ref[band, there, :] = (
                    mats_ref[3, plane, here, :] * strain_sq + mats_ref[4, plane, here, :] * dil_sq
                )
                stiff_sum = (
                    stiff_sum
                    + mats_ref[0, plane, here, :] * strain_sq
                    + mats_ref[1, plane, here, :] * dil_sq
                )
            acc_ref[band : band + 1] = sums_in_ref[band : band + 1] + jnp.sum(
                stiff_sum, axis=0, keepdims=True
            )
        acc_ref[bands : 2 * bands] = sums_in_ref[bands : 2 * bands]
        if last:
            sums_ref[...] = rows_to_lanes(jnp.sum(acc_ref[...], axis=1, keepdims=True), lanes)
        else:
            sums_ref[...] = acc_ref[...]

    return edge_kernel


def make_combine_kernel(cell_count, slabs, chunks):
    def combine_kernel(weights_ref, sums_a_ref, sums_b_ref, grad_ref, massd_ref, *refs):
        last_grad_refs = refs[: len(chunks)]
        ritz_ref, slab_refs = refs[len(chunks)], refs[len(chunks) + 1 :]
        bands, planes, rows, lanes = massd_ref.shape
        sums = sums_a_ref[...] + sums_b_ref[...]
        sums = jnp.broadcast_to(lanes_to_rows(sums, 2 * bands), (2 * bands, lanes))
        stiff = sums[0:bands]
        inert = sums[bands : 2 * bands]
        ritz = stiff / inert
        factor = weights_ref[...] * (cell_count / inert)
        tail = factor * ritz
        ritz_ref[...] = rows_to_lanes(ritz, lanes)[:, 0:bands]
        tiles = rows // ROWS // slabs
        me = lax.axis_index("ka") if slabs > 1 else 0
        for plane in range(planes):
            totals = []
            for begin in range(0, rows, ROWS):
                here = slice(begin, begin + ROWS)
                part = [i for i, (first, size) in enumerate(chunks) if first <= begin < first + size][0]
                there = slice(begin - chunks[part][0], begin - chunks[part][0] + ROWS)
                total = jnp.zeros((ROWS, lanes), F32)
                for band in range(bands):
                    if plane < planes - 1:
                        term = grad_ref[band, plane, here, :]
                    else:
                        term = last_grad_refs[part][band, there, :]
                    total = total + factor[band : band + 1] * term
                    total = total - tail[band : band + 1] * massd_ref[band, plane, here, :]
                totals.append(total)
            for at in range(slabs):
                for tile in range(tiles):
                    value = totals[at * tiles + tile]
                    for other in range(1, slabs):
                        value = jnp.where(me == other, totals[(at ^ other) * tiles + tile], value)
                    there = slice(tile * ROWS, (tile + 1) * ROWS)
                    if slabs == 4 and at % 2:
                        slab_refs[2][at // 2, plane, there, :] = value
                    else:
                        slab_refs[at // 2][plane, there, :] = value

    return combine_kernel


def on_device(band_fields, labels, phase_props, slopes, kpoints, rotations, band_weights):
    planes, rows, lanes = labels.shape
    bands = band_fields.shape[3]
    channels = 2 * bands
    gx_size = lax.axis_size("gx")
    gy_size = lax.axis_size("gy")
    ka_size = lax.axis_size("ka")
    cell_count = gx_size * gy_size * planes * rows * lanes
    params = pltpu.CompilerParams(vmem_limit_bytes=VMEM_LIMIT)

    chunks = row_chunks(rows)
    sliced, yrow = [], None
    for begin, size in chunks:
        behind = sliced[-1:] if yrow is None or len(sliced) > 1 else [yrow]
        sliced.append(
            pl.pallas_call(
                make_slice_kernel(begin, size, not sliced),
                out_shape=pltpu.VMEM((2, COMPS, bands, size, lanes), BF16),
                in_specs=[pl.BlockSpec(memory_space=pl.ANY)] + [vmem] * len(behind),
                out_specs=vmem,
                scratch_shapes=[pltpu.SemaphoreType.DMA(())],
                compiler_params=params,
                name="slice",
            )(band_fields, *[in_vmem(v) for v in behind])
        )
        if yrow is None:
            yrow = pl.pallas_call(
                edge_row_kernel,
                out_shape=pltpu.VMEM((COMPS, planes, channels, lanes), BF16),
                in_specs=[
                    pl.BlockSpec(
                        (1, 2, COMPS, bands, planes, ROWS, lanes), lambda i: (0, 0, 0, 0, 0, 0, 0)
                    ),
                    vmem,
                ],
                out_specs=pl.BlockSpec((COMPS, planes, channels, lanes), lambda i: (0, 0, 0, 0)),
                grid=(1,),
                compiler_params=params,
                name="edge_row",
            )(band_fields, in_vmem(sliced[0]))
    xplanes = [passed_along(value, "gx", -1) for value in sliced]
    yrow = passed_along(yrow, "gy", -1)

    spread, last_modes, grad, massd, strain, dil, sums, mats, weights = pl.pallas_call(
        interior_kernel,
        out_shape=(
            pltpu.VMEM((channels * ROWS, 3 * channels * ROWS), BF16),
            pltpu.VMEM((COMPS, channels, rows, lanes), F32),
            pltpu.VMEM((bands, planes - 1, rows, lanes), F32),
            pltpu.VMEM((bands, planes, rows, lanes), F32),
            pltpu.VMEM((bands, rows, lanes), F32),
            pltpu.VMEM((2, bands, rows, lanes), F32),
            pltpu.VMEM((2 * bands, lanes), F32),
            pltpu.VMEM((6, planes, rows, lanes), F32),
            pltpu.VMEM((bands, lanes), F32),
        ),
        in_specs=[smem, smem, smem, smem, vmem, vmem, vmem, vmem],
        out_specs=(vmem,) * 9,
        scratch_shapes=[
            pltpu.VMEM((planes, COMPS, channels, rows + 8, lanes), F32),
            pltpu.VMEM((2 * planes, bands, ROWS, lanes), F32),
            pltpu.VMEM((channels * ROWS, 3 * channels * ROWS), BF16),
        ],
        compiler_params=params,
        name="interior",
    )(kpoints.reshape(1, 1), phase_props, slopes, band_weights, rotations, labels, band_fields, in_vmem(yrow))

    last_grads = []
    for (begin, size), xplane in zip(chunks, xplanes):
        last = len(last_grads) == len(chunks) - 1
        last_grad, sums = pl.pallas_call(
            make_edge_kernel(begin, size, last),
            out_shape=(
                pltpu.VMEM((bands, size, lanes), F32),
                pltpu.VMEM((1 if last else 2 * bands, lanes), F32),
            ),
            in_specs=[vmem] * 7,
            out_specs=(vmem, vmem),
            scratch_shapes=[
                pltpu.VMEM((COMPS, channels, size, lanes), F32),
                pltpu.VMEM((2 * bands, lanes), F32),
            ],
            compiler_params=params,
            name="edge",
        )(*[in_vmem(v) for v in (mats, spread, last_modes, strain, dil, sums, xplane)])
        last_grads.append(last_grad)

    if is_power(gx_size) and is_power(gy_size) and gx_size > 1:
        steps = [("gy", 1 << i) for i in range(gy_size.bit_length() - 1)]
        steps += [("gx", 1 << i) for i in range(gx_size.bit_length() - 1)]
        for axis, flip in steps[:-1]:
            sums = sums + swapped(sums, axis, flip)
        other = swapped(sums, *steps[-1])
    else:
        sums = lax.psum(sums, ("gx", "gy"))
        other = jnp.zeros_like(sums)

    direct = ka_size == 4 and rows % (ROWS * ka_size) == 0
    slabs = ka_size if direct else 1
    slab = (planes, rows // slabs, lanes)
    slab_shapes = (slab, slab, (2,) + slab) if direct else (slab,)
    ritz, *pieces = pl.pallas_call(
        make_combine_kernel(float(cell_count), slabs, chunks),
        out_shape=(pltpu.VMEM((1, bands), F32),)
        + tuple(pltpu.VMEM(shape, F32) for shape in slab_shapes),
        in_specs=[vmem] * (5 + len(chunks)),
        out_specs=(vmem,) * (1 + len(slab_shapes)),
        compiler_params=params,
        name="combine",
    )(*[in_vmem(v) for v in (weights, sums, other, grad, massd, *last_grads)])
    if direct:
        own, far, away = pieces
        arrived = swapped(away, "ka", 1)
        design = own + arrived[0] + swapped(far + arrived[1], "ka", 2)
    else:
        design = lax.psum_scatter(pieces[0], "ka", scatter_dimension=1, tiled=True)
    return (ritz, design)


def solution(mesh):
    in_specs = (
        P("ka", None, None, None, "gx", "gy", None),
        P("gx", "gy", None),
        P(),
        P(),
        P("ka"),
        P("ka", None, None, None),
        P("ka", None),
    )
    out_specs = (P("ka", None), P("gx", ("gy", "ka"), None))
    return jax.shard_map(
        on_device, mesh=mesh, in_specs=in_specs, out_specs=out_specs, check_vma=False
    )
```

```python
import math

import jax
import jax.numpy as jnp
import numpy as np
from jax import lax
from jax.experimental import pallas as pl
from jax.experimental.pallas import tpu as pltpu
from jax.sharding import PartitionSpec as P

QGRID = 8
PHASES = 3
COMPS = 3
ROWS = 16
F32 = jnp.float32
BF16 = jnp.bfloat16
EXACT = lax.Precision.HIGHEST
VMEM_LIMIT = 56 * 1024 * 1024

vmem = pl.BlockSpec(memory_space=pltpu.VMEM)
smem = pl.BlockSpec(memory_space=pltpu.SMEM)


def in_vmem(value):
    return pltpu.with_memory_space_constraint(value, pltpu.VMEM)


def passed_along(value, axis, by):
    devices = lax.axis_size(axis)
    return lax.ppermute(value, axis, [(i, (i + by) % devices) for i in range(devices)])


def swapped(value, axis, flip):
    devices = lax.axis_size(axis)
    return lax.ppermute(value, axis, [(i, i ^ flip) for i in range(devices)])


def is_power(count):
    return count & (count - 1) == 0


def grid_turn(digit):
    angles = np.arange(QGRID, dtype=np.float32) * np.float32(2.0 * math.pi / QGRID)
    cosine, sine = jnp.float32(1.0), jnp.float32(0.0)
    for at in range(1, QGRID):
        cosine = jnp.where(digit == at, jnp.float32(np.cos(angles[at])), cosine)
        sine = jnp.where(digit == at, jnp.float32(np.sin(angles[at])), sine)
    return cosine, sine


def bf16_parts(value):
    high = value.astype(BF16)
    rest = value - high.astype(F32)
    middle = rest.astype(BF16)
    low = (rest - middle.astype(F32)).astype(BF16)
    return [high, middle, low]


def spread_rotation(real_part, imag_part, rows):
    bands = real_part.shape[0]
    wide = 2 * bands * rows
    tall_at = lax.broadcasted_iota(jnp.int32, (wide, bands), 0) // rows % bands
    tall = (tall_at == lax.broadcasted_iota(jnp.int32, (wide, bands), 1)).astype(F32)
    flat_at = lax.broadcasted_iota(jnp.int32, (bands, wide), 1) // rows % bands
    flat = (flat_at == lax.broadcasted_iota(jnp.int32, (bands, wide), 0)).astype(F32)

    def grown(matrix):
        tall_part = lax.dot_general(
            tall, matrix, (((1,), (1,)), ((), ())), precision=EXACT, preferred_element_type=F32
        )
        return jnp.dot(tall_part, flat, precision=EXACT, preferred_element_type=F32)

    row_at = lax.broadcasted_iota(jnp.int32, (wide, wide), 0)
    column_at = lax.broadcasted_iota(jnp.int32, (wide, wide), 1)
    row_half = row_at // (bands * rows)
    column_half = column_at // (bands * rows)
    real_grown = grown(real_part)
    imag_grown = grown(imag_part)
    imag_grown = jnp.where(row_half > column_half, imag_grown, -imag_grown)
    full = jnp.where(row_half == column_half, real_grown, imag_grown)
    full = jnp.where(row_at % rows == column_at % rows, full, 0.0)
    return jnp.concatenate(bf16_parts(full), axis=1)


def write_spread(out_ref, real_part, imag_part):
    bands = real_part.shape[0]
    half = bands * ROWS
    tall_at = lax.broadcasted_iota(jnp.int32, (half, bands), 0) // ROWS
    tall = (tall_at == lax.broadcasted_iota(jnp.int32, (half, bands), 1)).astype(BF16)
    flat_at = lax.broadcasted_iota(jnp.int32, (bands, half), 1) // ROWS
    flat = (flat_at == lax.broadcasted_iota(jnp.int32, (bands, half), 0)).astype(BF16)
    same_row = (lax.broadcasted_iota(jnp.int32, (half, half), 0) % ROWS) == (
        lax.broadcasted_iota(jnp.int32, (half, half), 1) % ROWS
    )

    def grown(part):
        tall_part = lax.dot_general(
            tall, part, (((1,), (1,)), ((), ())), preferred_element_type=F32
        ).astype(BF16)
        return jnp.where(same_row, jnp.dot(tall_part, flat, preferred_element_type=F32), 0.0)

    parts = zip(bf16_parts(real_part), bf16_parts(imag_part))
    for at, (real_bf16, imag_bf16) in enumerate(parts):
        real_grown, imag_grown = grown(real_bf16), grown(imag_bf16)
        left = slice(2 * at * half, (2 * at + 1) * half)
        right = slice((2 * at + 1) * half, (2 * at + 2) * half)
        out_ref[0:half, left] = real_grown.astype(BF16)
        out_ref[0:half, right] = (-imag_grown).astype(BF16)
        out_ref[half : 2 * half, left] = imag_grown.astype(BF16)
        out_ref[half : 2 * half, right] = real_grown.astype(BF16)


def row_chunks(rows):
    tiles = rows // ROWS
    sizes = [tiles - 1, 1] if tiles > 1 else [1]
    chunks, begin = [], 0
    for size in sizes:
        chunks.append((begin, size * ROWS))
        begin += size * ROWS
    return chunks


def turned_parts(real_part, imag_part, cosine, sine):
    return cosine * real_part - sine * imag_part, sine * real_part + cosine * imag_part


def picked(table, column, label_block):
    low = jnp.where(label_block == 0, table[0, column], table[1, column])
    return jnp.where(label_block == 2, table[2, column], low)


def rows_to_lanes(column, lanes):
    shape = (column.shape[0], lanes)
    diagonal = lax.broadcasted_iota(jnp.int32, shape, 0) == lax.broadcasted_iota(jnp.int32, shape, 1)
    return jnp.sum(jnp.where(diagonal, column, 0.0), axis=0, keepdims=True)


def lanes_to_rows(row, count):
    shape = (count, row.shape[1])
    diagonal = lax.broadcasted_iota(jnp.int32, shape, 0) == lax.broadcasted_iota(jnp.int32, shape, 1)
    return jnp.sum(jnp.where(diagonal, row, 0.0), axis=1, keepdims=True)


def make_slice_kernel(begin, size, in_steps):
    def slice_kernel(u_ref, *refs):
        out_ref, sem = refs[-2:]
        source = u_ref.at[0, :, :, :, 0, begin : begin + size]
        whole = pltpu.make_async_copy(source, out_ref, sem)
        if not in_steps:
            whole.start()
            whole.wait()
            return
        second = lax.axis_index("ka") % 2 == 1

        @pl.when(jnp.logical_not(second))
        def _():
            whole.start()
            whole.wait()

        @pl.when(second)
        def _():
            for band in range(out_ref.shape[2]):
                piece = pltpu.make_async_copy(source.at[:, :, band], out_ref.at[:, :, band], sem)
                piece.start()
                piece.wait()

    return slice_kernel


def edge_row_kernel(u_ref, after_ref, out_ref):
    planes = u_ref.shape[4]
    for comp in range(COMPS):
        for plane in range(planes):
            rows = u_ref[0, :, comp, :, plane, 0:1, :]
            out_ref[comp, plane] = rows.reshape(rows.shape[0] * rows.shape[1], rows.shape[3])


def interior_kernel(
    kpoint_ref,
    props_ref,
    slopes_ref,
    weights_in_ref,
    rotation_ref,
    labels_ref,
    u_ref,
    yrow_ref,
    spread_ref,
    last_modes_ref,
    grad_ref,
    massd_ref,
    strain_ref,
    dil_ref,
    sums_ref,
    mats_ref,
    weights_ref,
    modes_ref,
    acc_ref,
    own_ref,
):
    planes, rows, lanes = labels_ref.shape
    bands = u_ref.shape[3]
    channels = 2 * bands
    q_index = kpoint_ref[0, 0]
    band_at = lax.broadcasted_iota(jnp.int32, (bands, lanes), 0)
    weights = jnp.zeros((bands, lanes), F32)
    for band in range(bands):
        weights = jnp.where(band_at == band, weights_in_ref[0, band], weights)
    weights_ref[...] = weights
    x_last = lax.axis_index("gx") == lax.axis_size("gx") - 1
    y_last = lax.axis_index("gy") == lax.axis_size("gy") - 1
    x_turn = grid_turn(jnp.where(x_last, q_index // (QGRID * QGRID), 0))
    y_turn = grid_turn(jnp.where(y_last, q_index // QGRID % QGRID, 0))
    z_turn = grid_turn(q_index % QGRID)
    real_part, imag_part = rotation_ref[0, 0], rotation_ref[0, 1]
    write_spread(own_ref, real_part, imag_part)
    write_spread(spread_ref, *turned_parts(real_part, imag_part, *x_turn))
    spread_own = own_ref[...]
    edge_mix = spread_rotation(*turned_parts(real_part, imag_part, *y_turn), 1)
    for tile in range(rows // ROWS):
        here = slice(tile * ROWS, (tile + 1) * ROWS)
        for comp in range(COMPS):
            source = jnp.concatenate(
                [
                    u_ref[0, :, comp, :, plane, here, :].reshape(channels * ROWS, lanes)
                    for plane in range(planes)
                ],
                axis=1,
            )
            source = jnp.concatenate([source] * 3, axis=0)
            turned = jnp.dot(spread_own, source, preferred_element_type=F32)
            for plane in range(planes):
                part = turned[:, plane * lanes : (plane + 1) * lanes]
                part = part.reshape(channels, ROWS, lanes)
                modes_ref[plane, comp, :, here, :] = part
                if plane == planes - 1:
                    last_modes_ref[comp, :, here, :] = part
    for plane in range(planes):
        for comp in range(COMPS):
            edge = yrow_ref[comp, plane]
            edge = jnp.concatenate([edge] * 3, axis=0)
            edge = jnp.dot(edge_mix, edge, preferred_element_type=F32)
            modes_ref[plane, comp, :, rows : rows + 1, :] = edge[:, None, :]
        for column in range(3):
            mats_ref[column, plane] = picked(props_ref, column, labels_ref[plane])
            mats_ref[3 + column, plane] = picked(slopes_ref, column, labels_ref[plane])
    lane_at = lax.broadcasted_iota(jnp.int32, (ROWS, lanes), 1)
    is_end = lane_at == lanes - 1
    turn_cos = jnp.where(is_end, z_turn[0], 1.0)
    turn_sin = jnp.where(is_end, z_turn[1], 0.0)

    def per_band(band, carry):
        for plane in range(planes):
            inner = plane < planes - 1
            mass_sum = jnp.zeros((ROWS, lanes), F32)
            stiff_sum = jnp.zeros((ROWS, lanes), F32)
            for tile in range(rows // ROWS):
                begin = tile * ROWS
                here = slice(begin, begin + ROWS)
                after = slice(begin + 1, begin + 1 + ROWS)
                strain_sq = jnp.zeros((ROWS, lanes), F32)
                mass_sq = jnp.zeros((ROWS, lanes), F32)
                dil = [jnp.zeros((ROWS, lanes), F32)] * 2
                for comp in range(COMPS):
                    own = [modes_ref[plane, comp, t * bands + band, here, :] for t in range(2)]
                    roll = [pltpu.roll(v, lanes - 1, 1) for v in own]
                    along_z = [
                        turn_cos * roll[0] - turn_sin * roll[1],
                        turn_sin * roll[0] + turn_cos * roll[1],
                    ]
                    for t in range(2):
                        diff_z = along_z[t] - own[t]
                        diff_y = modes_ref[plane, comp, t * bands + band, after, :] - own[t]
                        strain_sq = strain_sq + diff_z * diff_z + diff_y * diff_y
                        if inner:
                            diff_x = (
                                modes_ref[plane + 1, comp, t * bands + band, here, :] - own[t]
                            )
                            strain_sq = strain_sq + diff_x * diff_x
                            if comp == 0:
                                dil[t] = dil[t] + diff_x
                        if comp == 1:
                            dil[t] = dil[t] + diff_y
                        if comp == 2:
                            dil[t] = dil[t] + diff_z
                        mass_sq = mass_sq + own[t] * own[t]
                mass_sum = mass_sum + mats_ref[2, plane, here, :] * mass_sq
                massd_ref[band, plane, here, :] = mats_ref[5, plane, here, :] * mass_sq
                if inner:
                    dil_sq = dil[0] * dil[0] + dil[1] * dil[1]
                    stiff_sum = (
                        stiff_sum
                        + mats_ref[0, plane, here, :] * strain_sq
                        + mats_ref[1, plane, here, :] * dil_sq
                    )
                    grad_ref[band, plane, here, :] = (
                        mats_ref[3, plane, here, :] * strain_sq
                        + mats_ref[4, plane, here, :] * dil_sq
                    )
                else:
                    strain_ref[band, here, :] = strain_sq
                    dil_ref[0, band, here, :] = dil[0]
                    dil_ref[1, band, here, :] = dil[1]
            acc_ref[plane, band] = stiff_sum
            acc_ref[planes + plane, band] = mass_sum
        return carry

    lax.fori_loop(0, bands, per_band, 0)
    sums_ref[0:bands] = jnp.sum(jnp.sum(acc_ref[0:planes], axis=0), axis=1)
    sums_ref[bands : 2 * bands] = jnp.sum(jnp.sum(acc_ref[planes : 2 * planes], axis=0), axis=1)


def make_edge_kernel(begin, size, last):
    def edge_kernel(
        mats_ref,
        spread_ref,
        modes_ref,
        strain_ref,
        dil_ref,
        sums_in_ref,
        plane_ref,
        grad_ref,
        sums_ref,
        next_ref,
        acc_ref,
    ):
        bands, _, lanes = strain_ref.shape
        channels = 2 * bands
        tiles = size // ROWS
        blocks = [(comp, tile) for comp in range(COMPS) for tile in range(tiles)]
        source = jnp.concatenate(
            [
                plane_ref[:, comp, :, tile * ROWS : (tile + 1) * ROWS, :].reshape(
                    channels * ROWS, lanes
                )
                for comp, tile in blocks
            ],
            axis=1,
        )
        source = jnp.concatenate([source] * 3, axis=0)
        turned = jnp.dot(spread_ref[...], source, preferred_element_type=F32)
        for at, (comp, tile) in enumerate(blocks):
            next_ref[comp, :, tile * ROWS : (tile + 1) * ROWS, :] = turned[
                :, at * lanes : (at + 1) * lanes
            ].reshape(channels, ROWS, lanes)
        plane = mats_ref.shape[1] - 1
        for band in range(bands):
            stiff_sum = jnp.zeros((ROWS, lanes), F32)
            for tile in range(tiles):
                here = slice(begin + tile * ROWS, begin + (tile + 1) * ROWS)
                there = slice(tile * ROWS, (tile + 1) * ROWS)
                strain_sq = strain_ref[band, here, :]
                dil = [dil_ref[t, band, here, :] for t in range(2)]
                for comp in range(COMPS):
                    for t in range(2):
                        diff_x = (
                            next_ref[comp, t * bands + band, there, :]
                            - modes_ref[comp, t * bands + band, here, :]
                        )
                        strain_sq = strain_sq + diff_x * diff_x
                        if comp == 0:
                            dil[t] = dil[t] + diff_x
                dil_sq = dil[0] * dil[0] + dil[1] * dil[1]
                grad_ref[band, there, :] = (
                    mats_ref[3, plane, here, :] * strain_sq + mats_ref[4, plane, here, :] * dil_sq
                )
                stiff_sum = (
                    stiff_sum
                    + mats_ref[0, plane, here, :] * strain_sq
                    + mats_ref[1, plane, here, :] * dil_sq
                )
            acc_ref[band : band + 1] = sums_in_ref[band : band + 1] + jnp.sum(
                stiff_sum, axis=0, keepdims=True
            )
        acc_ref[bands : 2 * bands] = sums_in_ref[bands : 2 * bands]
        if last:
            sums_ref[...] = rows_to_lanes(jnp.sum(acc_ref[...], axis=1, keepdims=True), lanes)
        else:
            sums_ref[...] = acc_ref[...]

    return edge_kernel


def make_combine_kernel(cell_count, slabs, chunks):
    def combine_kernel(weights_ref, sums_a_ref, sums_b_ref, grad_ref, massd_ref, *refs):
        last_grad_refs = refs[: len(chunks)]
        ritz_ref, slab_refs = refs[len(chunks)], refs[len(chunks) + 1 :]
        bands, planes, rows, lanes = massd_ref.shape
        sums = sums_a_ref[...] + sums_b_ref[...]
        sums = jnp.broadcast_to(lanes_to_rows(sums, 2 * bands), (2 * bands, lanes))
        stiff = sums[0:bands]
        inert = sums[bands : 2 * bands]
        ritz = stiff / inert
        factor = weights_ref[...] * (cell_count / inert)
        tail = factor * ritz
        ritz_ref[...] = rows_to_lanes(ritz, lanes)[:, 0:bands]
        tiles = rows // ROWS // slabs
        me = lax.axis_index("ka") if slabs > 1 else 0
        for plane in range(planes):
            totals = []
            for begin in range(0, rows, ROWS):
                here = slice(begin, begin + ROWS)
                part = [i for i, (first, size) in enumerate(chunks) if first <= begin < first + size][0]
                there = slice(begin - chunks[part][0], begin - chunks[part][0] + ROWS)
                total = jnp.zeros((ROWS, lanes), F32)
                for band in range(bands):
                    if plane < planes - 1:
                        term = grad_ref[band, plane, here, :]
                    else:
                        term = last_grad_refs[part][band, there, :]
                    total = total + factor[band : band + 1] * term
                    total = total - tail[band : band + 1] * massd_ref[band, plane, here, :]
                totals.append(total)
            for at in range(slabs):
                for tile in range(tiles):
                    value = totals[at * tiles + tile]
                    for other in range(1, slabs):
                        value = jnp.where(me == other, totals[(at ^ other) * tiles + tile], value)
                    there = slice(tile * ROWS, (tile + 1) * ROWS)
                    if at >= 2:
                        slab_refs[2][at - 2, plane, there, :] = value
                    else:
                        slab_refs[at][plane, there, :] = value

    return combine_kernel


def on_device(band_fields, labels, phase_props, slopes, kpoints, rotations, band_weights):
    planes, rows, lanes = labels.shape
    bands = band_fields.shape[3]
    channels = 2 * bands
    gx_size = lax.axis_size("gx")
    gy_size = lax.axis_size("gy")
    ka_size = lax.axis_size("ka")
    cell_count = gx_size * gy_size * planes * rows * lanes
    params = pltpu.CompilerParams(vmem_limit_bytes=VMEM_LIMIT)

    chunks = row_chunks(rows)
    sliced, yrow = [], None
    for begin, size in chunks:
        behind = sliced[-1:] if yrow is None or len(sliced) > 1 else [yrow]
        sliced.append(
            pl.pallas_call(
                make_slice_kernel(begin, size, not sliced),
                out_shape=pltpu.VMEM((2, COMPS, bands, size, lanes), BF16),
                in_specs=[pl.BlockSpec(memory_space=pl.ANY)] + [vmem] * len(behind),
                out_specs=vmem,
                scratch_shapes=[pltpu.SemaphoreType.DMA(())],
                compiler_params=params,
                name="slice",
            )(band_fields, *[in_vmem(v) for v in behind])
        )
        if yrow is None:
            yrow = pl.pallas_call(
                edge_row_kernel,
                out_shape=pltpu.VMEM((COMPS, planes, channels, lanes), BF16),
                in_specs=[
                    pl.BlockSpec(
                        (1, 2, COMPS, bands, planes, ROWS, lanes), lambda i: (0, 0, 0, 0, 0, 0, 0)
                    ),
                    vmem,
                ],
                out_specs=pl.BlockSpec((COMPS, planes, channels, lanes), lambda i: (0, 0, 0, 0)),
                grid=(1,),
                compiler_params=params,
                name="edge_row",
            )(band_fields, in_vmem(sliced[0]))
    xplanes = [passed_along(value, "gx", -1) for value in sliced]
    yrow = passed_along(yrow, "gy", -1)

    spread, last_modes, grad, massd, strain, dil, sums, mats, weights = pl.pallas_call(
        interior_kernel,
        out_shape=(
            pltpu.VMEM((channels * ROWS, 3 * channels * ROWS), BF16),
            pltpu.VMEM((COMPS, channels, rows, lanes), F32),
            pltpu.VMEM((bands, planes - 1, rows, lanes), F32),
            pltpu.VMEM((bands, planes, rows, lanes), F32),
            pltpu.VMEM((bands, rows, lanes), F32),
            pltpu.VMEM((2, bands, rows, lanes), F32),
            pltpu.VMEM((2 * bands, lanes), F32),
            pltpu.VMEM((6, planes, rows, lanes), F32),
            pltpu.VMEM((bands, lanes), F32),
        ),
        in_specs=[smem, smem, smem, smem, vmem, vmem, vmem, vmem],
        out_specs=(vmem,) * 9,
        scratch_shapes=[
            pltpu.VMEM((planes, COMPS, channels, rows + 8, lanes), F32),
            pltpu.VMEM((2 * planes, bands, ROWS, lanes), F32),
            pltpu.VMEM((channels * ROWS, 3 * channels * ROWS), BF16),
        ],
        compiler_params=params,
        name="interior",
    )(kpoints.reshape(1, 1), phase_props, slopes, band_weights, rotations, labels, band_fields, in_vmem(yrow))

    last_grads = []
    for (begin, size), xplane in zip(chunks, xplanes):
        last = len(last_grads) == len(chunks) - 1
        last_grad, sums = pl.pallas_call(
            make_edge_kernel(begin, size, last),
            out_shape=(
                pltpu.VMEM((bands, size, lanes), F32),
                pltpu.VMEM((1 if last else 2 * bands, lanes), F32),
            ),
            in_specs=[vmem] * 7,
            out_specs=(vmem, vmem),
            scratch_shapes=[
                pltpu.VMEM((COMPS, channels, size, lanes), F32),
                pltpu.VMEM((2 * bands, lanes), F32),
            ],
            compiler_params=params,
            name="edge",
        )(*[in_vmem(v) for v in (mats, spread, last_modes, strain, dil, sums, xplane)])
        last_grads.append(last_grad)

    if is_power(gx_size) and is_power(gy_size) and gx_size > 1:
        steps = [("gy", 1 << i) for i in range(gy_size.bit_length() - 1)]
        steps += [("gx", 1 << i) for i in range(gx_size.bit_length() - 1)]
        for axis, flip in steps[:-1]:
            sums = sums + swapped(sums, axis, flip)
        other = swapped(sums, *steps[-1])
    else:
        sums = lax.psum(sums, ("gx", "gy"))
        other = jnp.zeros_like(sums)

    direct = ka_size == 4 and rows % (ROWS * ka_size) == 0
    slabs = ka_size if direct else 1
    slab = (planes, rows // slabs, lanes)
    slab_shapes = (slab, slab, (2,) + slab) if direct else (slab,)
    ritz, *pieces = pl.pallas_call(
        make_combine_kernel(float(cell_count), slabs, chunks),
        out_shape=(pltpu.VMEM((1, bands), F32),)
        + tuple(pltpu.VMEM(shape, F32) for shape in slab_shapes),
        in_specs=[vmem] * (5 + len(chunks)),
        out_specs=(vmem,) * (1 + len(slab_shapes)),
        compiler_params=params,
        name="combine",
    )(*[in_vmem(v) for v in (weights, sums, other, grad, massd, *last_grads)])
    if direct:
        own, near, far = pieces
        arrived = swapped(far, "ka", 2)
        design = own + arrived[0] + swapped(near + arrived[1], "ka", 1)
    else:
        design = lax.psum_scatter(pieces[0], "ka", scatter_dimension=1, tiled=True)
    return (ritz, design)


def solution(mesh):
    in_specs = (
        P("ka", None, None, None, "gx", "gy", None),
        P("gx", "gy", None),
        P(),
        P(),
        P("ka"),
        P("ka", None, None, None),
        P("ka", None),
    )
    out_specs = (P("ka", None), P("gx", ("gy", "ka"), None))
    return jax.shard_map(
        on_device, mesh=mesh, in_specs=in_specs, out_specs=out_specs, check_vma=False
    )
```

```python
import math

import jax
import jax.numpy as jnp
import numpy as np
from jax import lax
from jax.experimental import pallas as pl
from jax.experimental.pallas import tpu as pltpu
from jax.sharding import PartitionSpec as P

QGRID = 8
PHASES = 3
COMPS = 3
ROWS = 16
F32 = jnp.float32
BF16 = jnp.bfloat16
EXACT = lax.Precision.HIGHEST
VMEM_LIMIT = 56 * 1024 * 1024

vmem = pl.BlockSpec(memory_space=pltpu.VMEM)
smem = pl.BlockSpec(memory_space=pltpu.SMEM)


def in_vmem(value):
    return pltpu.with_memory_space_constraint(value, pltpu.VMEM)


def passed_along(value, axis, by):
    devices = lax.axis_size(axis)
    return lax.ppermute(value, axis, [(i, (i + by) % devices) for i in range(devices)])


def swapped(value, axis, flip):
    devices = lax.axis_size(axis)
    return lax.ppermute(value, axis, [(i, i ^ flip) for i in range(devices)])


def is_power(count):
    return count & (count - 1) == 0


def grid_turn(digit):
    angles = np.arange(QGRID, dtype=np.float32) * np.float32(2.0 * math.pi / QGRID)
    cosine, sine = jnp.float32(1.0), jnp.float32(0.0)
    for at in range(1, QGRID):
        cosine = jnp.where(digit == at, jnp.float32(np.cos(angles[at])), cosine)
        sine = jnp.where(digit == at, jnp.float32(np.sin(angles[at])), sine)
    return cosine, sine


def bf16_parts(value):
    high = value.astype(BF16)
    rest = value - high.astype(F32)
    middle = rest.astype(BF16)
    low = (rest - middle.astype(F32)).astype(BF16)
    return [high, middle, low]


def spread_rotation(real_part, imag_part, rows):
    bands = real_part.shape[0]
    wide = 2 * bands * rows
    tall_at = lax.broadcasted_iota(jnp.int32, (wide, bands), 0) // rows % bands
    tall = (tall_at == lax.broadcasted_iota(jnp.int32, (wide, bands), 1)).astype(F32)
    flat_at = lax.broadcasted_iota(jnp.int32, (bands, wide), 1) // rows % bands
    flat = (flat_at == lax.broadcasted_iota(jnp.int32, (bands, wide), 0)).astype(F32)

    def grown(matrix):
        tall_part = lax.dot_general(
            tall, matrix, (((1,), (1,)), ((), ())), precision=EXACT, preferred_element_type=F32
        )
        return jnp.dot(tall_part, flat, precision=EXACT, preferred_element_type=F32)

    row_at = lax.broadcasted_iota(jnp.int32, (wide, wide), 0)
    column_at = lax.broadcasted_iota(jnp.int32, (wide, wide), 1)
    row_half = row_at // (bands * rows)
    column_half = column_at // (bands * rows)
    real_grown = grown(real_part)
    imag_grown = grown(imag_part)
    imag_grown = jnp.where(row_half > column_half, imag_grown, -imag_grown)
    full = jnp.where(row_half == column_half, real_grown, imag_grown)
    full = jnp.where(row_at % rows == column_at % rows, full, 0.0)
    return jnp.concatenate(bf16_parts(full), axis=1)


def write_spread(out_ref, real_part, imag_part):
    bands = real_part.shape[0]
    half = bands * ROWS
    tall_at = lax.broadcasted_iota(jnp.int32, (half, bands), 0) // ROWS
    tall = (tall_at == lax.broadcasted_iota(jnp.int32, (half, bands), 1)).astype(BF16)
    flat_at = lax.broadcasted_iota(jnp.int32, (bands, half), 1) // ROWS
    flat = (flat_at == lax.broadcasted_iota(jnp.int32, (bands, half), 0)).astype(BF16)
    same_row = (lax.broadcasted_iota(jnp.int32, (half, half), 0) % ROWS) == (
        lax.broadcasted_iota(jnp.int32, (half, half), 1) % ROWS
    )

    def grown(part):
        tall_part = lax.dot_general(
            tall, part, (((1,), (1,)), ((), ())), preferred_element_type=F32
        ).astype(BF16)
        return jnp.where(same_row, jnp.dot(tall_part, flat, preferred_element_type=F32), 0.0)

    parts = zip(bf16_parts(real_part), bf16_parts(imag_part))
    for at, (real_bf16, imag_bf16) in enumerate(parts):
        real_grown, imag_grown = grown(real_bf16), grown(imag_bf16)
        left = slice(2 * at * half, (2 * at + 1) * half)
        right = slice((2 * at + 1) * half, (2 * at + 2) * half)
        out_ref[0:half, left] = real_grown.astype(BF16)
        out_ref[0:half, right] = (-imag_grown).astype(BF16)
        out_ref[half : 2 * half, left] = imag_grown.astype(BF16)
        out_ref[half : 2 * half, right] = real_grown.astype(BF16)


def row_chunks(rows):
    tiles = rows // ROWS
    sizes = [tiles - 1, 1] if tiles > 1 else [1]
    chunks, begin = [], 0
    for size in sizes:
        chunks.append((begin, size * ROWS))
        begin += size * ROWS
    return chunks


def turned_parts(real_part, imag_part, cosine, sine):
    return cosine * real_part - sine * imag_part, sine * real_part + cosine * imag_part


def picked(table, column, label_block):
    low = jnp.where(label_block == 0, table[0, column], table[1, column])
    return jnp.where(label_block == 2, table[2, column], low)


def rows_to_lanes(column, lanes):
    shape = (column.shape[0], lanes)
    diagonal = lax.broadcasted_iota(jnp.int32, shape, 0) == lax.broadcasted_iota(jnp.int32, shape, 1)
    return jnp.sum(jnp.where(diagonal, column, 0.0), axis=0, keepdims=True)


def lanes_to_rows(row, count):
    shape = (count, row.shape[1])
    diagonal = lax.broadcasted_iota(jnp.int32, shape, 0) == lax.broadcasted_iota(jnp.int32, shape, 1)
    return jnp.sum(jnp.where(diagonal, row, 0.0), axis=1, keepdims=True)


def make_slice_kernel(begin, size, in_steps):
    def slice_kernel(u_ref, *refs):
        out_ref, sem = refs[-2:]
        source = u_ref.at[0, :, :, :, 0, begin : begin + size]
        whole = pltpu.make_async_copy(source, out_ref, sem)
        if not in_steps:
            whole.start()
            whole.wait()
            return
        second = lax.axis_index("ka") % 2 == 1

        @pl.when(jnp.logical_not(second))
        def _():
            whole.start()
            whole.wait()

        @pl.when(second)
        def _():
            for band in range(out_ref.shape[2]):
                piece = pltpu.make_async_copy(source.at[:, :, band], out_ref.at[:, :, band], sem)
                piece.start()
                piece.wait()

    return slice_kernel


def edge_row_kernel(u_ref, after_ref, out_ref):
    planes = u_ref.shape[4]
    for comp in range(COMPS):
        for plane in range(planes):
            tile = u_ref[0, :, comp, :, plane, :, :].astype(F32)
            rows = tile.reshape(tile.shape[0] * tile.shape[1], ROWS, tile.shape[3])[:, 0, :]
            out_ref[comp, plane] = rows.astype(BF16)


def interior_kernel(
    kpoint_ref,
    props_ref,
    slopes_ref,
    weights_in_ref,
    rotation_ref,
    labels_ref,
    u_ref,
    yrow_ref,
    spread_ref,
    last_modes_ref,
    grad_ref,
    massd_ref,
    strain_ref,
    dil_ref,
    sums_ref,
    mats_ref,
    weights_ref,
    modes_ref,
    acc_ref,
    own_ref,
):
    planes, rows, lanes = labels_ref.shape
    bands = u_ref.shape[3]
    channels = 2 * bands
    q_index = kpoint_ref[0, 0]
    band_at = lax.broadcasted_iota(jnp.int32, (bands, lanes), 0)
    weights = jnp.zeros((bands, lanes), F32)
    for band in range(bands):
        weights = jnp.where(band_at == band, weights_in_ref[0, band], weights)
    weights_ref[...] = weights
    x_last = lax.axis_index("gx") == lax.axis_size("gx") - 1
    y_last = lax.axis_index("gy") == lax.axis_size("gy") - 1
    x_turn = grid_turn(jnp.where(x_last, q_index // (QGRID * QGRID), 0))
    y_turn = grid_turn(jnp.where(y_last, q_index // QGRID % QGRID, 0))
    z_turn = grid_turn(q_index % QGRID)
    real_part, imag_part = rotation_ref[0, 0], rotation_ref[0, 1]
    write_spread(own_ref, real_part, imag_part)
    write_spread(spread_ref, *turned_parts(real_part, imag_part, *x_turn))
    spread_own = own_ref[...]
    edge_mix = spread_rotation(*turned_parts(real_part, imag_part, *y_turn), 1)
    for tile in range(rows // ROWS):
        here = slice(tile * ROWS, (tile + 1) * ROWS)
        for comp in range(COMPS):
            source = jnp.concatenate(
                [
                    u_ref[0, :, comp, :, plane, here, :].reshape(channels * ROWS, lanes)
                    for plane in range(planes)
                ],
                axis=1,
            )
            source = jnp.concatenate([source] * 3, axis=0)
            turned = jnp.dot(spread_own, source, preferred_element_type=F32)
            for plane in range(planes):
                part = turned[:, plane * lanes : (plane + 1) * lanes]
                part = part.reshape(channels, ROWS, lanes)
                modes_ref[plane, comp, :, here, :] = part
                if plane == planes - 1:
                    last_modes_ref[comp, :, here, :] = part
    for plane in range(planes):
        for comp in range(COMPS):
            edge = yrow_ref[comp, plane]
            edge = jnp.concatenate([edge] * 3, axis=0)
            edge = jnp.dot(edge_mix, edge, preferred_element_type=F32)
            modes_ref[plane, comp, :, rows : rows + 1, :] = edge[:, None, :]
        for column in range(3):
            mats_ref[column, plane] = picked(props_ref, column, labels_ref[plane])
            mats_ref[3 + column, plane] = picked(slopes_ref, column, labels_ref[plane])
    lane_at = lax.broadcasted_iota(jnp.int32, (ROWS, lanes), 1)
    is_end = lane_at == lanes - 1
    turn_cos = jnp.where(is_end, z_turn[0], 1.0)
    turn_sin = jnp.where(is_end, z_turn[1], 0.0)

    def per_band(band, carry):
        for plane in range(planes):
            inner = plane < planes - 1
            mass_sum = jnp.zeros((ROWS, lanes), F32)
            stiff_sum = jnp.zeros((ROWS, lanes), F32)
            for tile in range(rows // ROWS):
                begin = tile * ROWS
                here = slice(begin, begin + ROWS)
                after = slice(begin + 1, begin + 1 + ROWS)
                strain_sq = jnp.zeros((ROWS, lanes), F32)
                mass_sq = jnp.zeros((ROWS, lanes), F32)
                dil = [jnp.zeros((ROWS, lanes), F32)] * 2
                for comp in range(COMPS):
                    own = [modes_ref[plane, comp, t * bands + band, here, :] for t in range(2)]
                    roll = [pltpu.roll(v, lanes - 1, 1) for v in own]
                    along_z = [
                        turn_cos * roll[0] - turn_sin * roll[1],
                        turn_sin * roll[0] + turn_cos * roll[1],
                    ]
                    for t in range(2):
                        diff_z = along_z[t] - own[t]
                        diff_y = modes_ref[plane, comp, t * bands + band, after, :] - own[t]
                        strain_sq = strain_sq + diff_z * diff_z + diff_y * diff_y
                        if inner:
                            diff_x = (
                                modes_ref[plane + 1, comp, t * bands + band, here, :] - own[t]
                            )
                            strain_sq = strain_sq + diff_x * diff_x
                            if comp == 0:
                                dil[t] = dil[t] + diff_x
                        if comp == 1:
                            dil[t] = dil[t] + diff_y
                        if comp == 2:
                            dil[t] = dil[t] + diff_z
                        mass_sq = mass_sq + own[t] * own[t]
                mass_sum = mass_sum + mats_ref[2, plane, here, :] * mass_sq
                massd_ref[band, plane, here, :] = mats_ref[5, plane, here, :] * mass_sq
                if inner:
                    dil_sq = dil[0] * dil[0] + dil[1] * dil[1]
                    stiff_sum = (
                        stiff_sum
                        + mats_ref[0, plane, here, :] * strain_sq
                        + mats_ref[1, plane, here, :] * dil_sq
                    )
                    grad_ref[band, plane, here, :] = (
                        mats_ref[3, plane, here, :] * strain_sq
                        + mats_ref[4, plane, here, :] * dil_sq
                    )
                else:
                    strain_ref[band, here, :] = strain_sq
                    dil_ref[0, band, here, :] = dil[0]
                    dil_ref[1, band, here, :] = dil[1]
            acc_ref[plane, band] = stiff_sum
            acc_ref[planes + plane, band] = mass_sum
        return carry

    lax.fori_loop(0, bands, per_band, 0)
    sums_ref[0:bands] = jnp.sum(jnp.sum(acc_ref[0:planes], axis=0), axis=1)
    sums_ref[bands : 2 * bands] = jnp.sum(jnp.sum(acc_ref[planes : 2 * planes], axis=0), axis=1)


def make_edge_kernel(begin, size, last):
    def edge_kernel(
        mats_ref,
        spread_ref,
        modes_ref,
        strain_ref,
        dil_ref,
        sums_in_ref,
        plane_ref,
        grad_ref,
        sums_ref,
        next_ref,
        acc_ref,
    ):
        bands, _, lanes = strain_ref.shape
        channels = 2 * bands
        tiles = size // ROWS
        blocks = [(comp, tile) for comp in range(COMPS) for tile in range(tiles)]
        source = jnp.concatenate(
            [
                plane_ref[:, comp, :, tile * ROWS : (tile + 1) * ROWS, :].reshape(
                    channels * ROWS, lanes
                )
                for comp, tile in blocks
            ],
            axis=1,
        )
        source = jnp.concatenate([source] * 3, axis=0)
        turned = jnp.dot(spread_ref[...], source, preferred_element_type=F32)
        for at, (comp, tile) in enumerate(blocks):
            next_ref[comp, :, tile * ROWS : (tile + 1) * ROWS, :] = turned[
                :, at * lanes : (at + 1) * lanes
            ].reshape(channels, ROWS, lanes)
        plane = mats_ref.shape[1] - 1
        for band in range(bands):
            stiff_sum = jnp.zeros((ROWS, lanes), F32)
            for tile in range(tiles):
                here = slice(begin + tile * ROWS, begin + (tile + 1) * ROWS)
                there = slice(tile * ROWS, (tile + 1) * ROWS)
                strain_sq = strain_ref[band, here, :]
                dil = [dil_ref[t, band, here, :] for t in range(2)]
                for comp in range(COMPS):
                    for t in range(2):
                        diff_x = (
                            next_ref[comp, t * bands + band, there, :]
                            - modes_ref[comp, t * bands + band, here, :]
                        )
                        strain_sq = strain_sq + diff_x * diff_x
                        if comp == 0:
                            dil[t] = dil[t] + diff_x
                dil_sq = dil[0] * dil[0] + dil[1] * dil[1]
                grad_ref[band, there, :] = (
                    mats_ref[3, plane, here, :] * strain_sq + mats_ref[4, plane, here, :] * dil_sq
                )
                stiff_sum = (
                    stiff_sum
                    + mats_ref[0, plane, here, :] * strain_sq
                    + mats_ref[1, plane, here, :] * dil_sq
                )
            acc_ref[band : band + 1] = sums_in_ref[band : band + 1] + jnp.sum(
                stiff_sum, axis=0, keepdims=True
            )
        acc_ref[bands : 2 * bands] = sums_in_ref[bands : 2 * bands]
        if last:
            sums_ref[...] = rows_to_lanes(jnp.sum(acc_ref[...], axis=1, keepdims=True), lanes)
        else:
            sums_ref[...] = acc_ref[...]

    return edge_kernel


def make_combine_kernel(cell_count, slabs, chunks):
    def combine_kernel(weights_ref, sums_a_ref, sums_b_ref, grad_ref, massd_ref, *refs):
        last_grad_refs = refs[: len(chunks)]
        ritz_ref, slab_refs = refs[len(chunks)], refs[len(chunks) + 1 :]
        bands, planes, rows, lanes = massd_ref.shape
        sums = sums_a_ref[...] + sums_b_ref[...]
        sums = jnp.broadcast_to(lanes_to_rows(sums, 2 * bands), (2 * bands, lanes))
        stiff = sums[0:bands]
        inert = sums[bands : 2 * bands]
        ritz = stiff / inert
        factor = weights_ref[...] * (cell_count / inert)
        tail = factor * ritz
        ritz_ref[...] = rows_to_lanes(ritz, lanes)[:, 0:bands]
        tiles = rows // ROWS // slabs
        me = lax.axis_index("ka") if slabs > 1 else 0
        for plane in range(planes):
            totals = []
            for begin in range(0, rows, ROWS):
                here = slice(begin, begin + ROWS)
                part = [i for i, (first, size) in enumerate(chunks) if first <= begin < first + size][0]
                there = slice(begin - chunks[part][0], begin - chunks[part][0] + ROWS)
                total = jnp.zeros((ROWS, lanes), F32)
                for band in range(bands):
                    if plane < planes - 1:
                        term = grad_ref[band, plane, here, :]
                    else:
                        term = last_grad_refs[part][band, there, :]
                    total = total + factor[band : band + 1] * term
                    total = total - tail[band : band + 1] * massd_ref[band, plane, here, :]
                totals.append(total)
            for at in range(slabs):
                for tile in range(tiles):
                    value = totals[at * tiles + tile]
                    for other in range(1, slabs):
                        value = jnp.where(me == other, totals[(at ^ other) * tiles + tile], value)
                    there = slice(tile * ROWS, (tile + 1) * ROWS)
                    if at >= 2:
                        slab_refs[2][at - 2, plane, there, :] = value
                    else:
                        slab_refs[at][plane, there, :] = value

    return combine_kernel


def on_device(band_fields, labels, phase_props, slopes, kpoints, rotations, band_weights):
    planes, rows, lanes = labels.shape
    bands = band_fields.shape[3]
    channels = 2 * bands
    gx_size = lax.axis_size("gx")
    gy_size = lax.axis_size("gy")
    ka_size = lax.axis_size("ka")
    cell_count = gx_size * gy_size * planes * rows * lanes
    params = pltpu.CompilerParams(vmem_limit_bytes=VMEM_LIMIT)

    chunks = row_chunks(rows)
    sliced, yrow = [], None
    for begin, size in chunks:
        behind = sliced[-1:] if yrow is None or len(sliced) > 1 else [yrow]
        sliced.append(
            pl.pallas_call(
                make_slice_kernel(begin, size, not sliced),
                out_shape=pltpu.VMEM((2, COMPS, bands, size, lanes), BF16),
                in_specs=[pl.BlockSpec(memory_space=pl.ANY)] + [vmem] * len(behind),
                out_specs=vmem,
                scratch_shapes=[pltpu.SemaphoreType.DMA(())],
                compiler_params=params,
                name="slice",
            )(band_fields, *[in_vmem(v) for v in behind])
        )
        if yrow is None:
            yrow = pl.pallas_call(
                edge_row_kernel,
                out_shape=pltpu.VMEM((COMPS, planes, channels, lanes), BF16),
                in_specs=[
                    pl.BlockSpec(
                        (1, 2, COMPS, bands, planes, ROWS, lanes), lambda i: (0, 0, 0, 0, 0, 0, 0)
                    ),
                    vmem,
                ],
                out_specs=pl.BlockSpec((COMPS, planes, channels, lanes), lambda i: (0, 0, 0, 0)),
                grid=(1,),
                compiler_params=params,
                name="edge_row",
            )(band_fields, in_vmem(sliced[0]))
    xplanes = [passed_along(value, "gx", -1) for value in sliced]
    yrow = passed_along(yrow, "gy", -1)

    spread, last_modes, grad, massd, strain, dil, sums, mats, weights = pl.pallas_call(
        interior_kernel,
        out_shape=(
            pltpu.VMEM((channels * ROWS, 3 * channels * ROWS), BF16),
            pltpu.VMEM((COMPS, channels, rows, lanes), F32),
            pltpu.VMEM((bands, planes - 1, rows, lanes), F32),
            pltpu.VMEM((bands, planes, rows, lanes), F32),
            pltpu.VMEM((bands, rows, lanes), F32),
            pltpu.VMEM((2, bands, rows, lanes), F32),
            pltpu.VMEM((2 * bands, lanes), F32),
            pltpu.VMEM((6, planes, rows, lanes), F32),
            pltpu.VMEM((bands, lanes), F32),
        ),
        in_specs=[smem, smem, smem, smem, vmem, vmem, vmem, vmem],
        out_specs=(vmem,) * 9,
        scratch_shapes=[
            pltpu.VMEM((planes, COMPS, channels, rows + 8, lanes), F32),
            pltpu.VMEM((2 * planes, bands, ROWS, lanes), F32),
            pltpu.VMEM((channels * ROWS, 3 * channels * ROWS), BF16),
        ],
        compiler_params=params,
        name="interior",
    )(kpoints.reshape(1, 1), phase_props, slopes, band_weights, rotations, labels, band_fields, in_vmem(yrow))

    last_grads = []
    for (begin, size), xplane in zip(chunks, xplanes):
        last = len(last_grads) == len(chunks) - 1
        last_grad, sums = pl.pallas_call(
            make_edge_kernel(begin, size, last),
            out_shape=(
                pltpu.VMEM((bands, size, lanes), F32),
                pltpu.VMEM((1 if last else 2 * bands, lanes), F32),
            ),
            in_specs=[vmem] * 7,
            out_specs=(vmem, vmem),
            scratch_shapes=[
                pltpu.VMEM((COMPS, channels, size, lanes), F32),
                pltpu.VMEM((2 * bands, lanes), F32),
            ],
            compiler_params=params,
            name="edge",
        )(*[in_vmem(v) for v in (mats, spread, last_modes, strain, dil, sums, xplane)])
        last_grads.append(last_grad)

    if is_power(gx_size) and is_power(gy_size) and gx_size > 1:
        steps = [("gy", 1 << i) for i in range(gy_size.bit_length() - 1)]
        steps += [("gx", 1 << i) for i in range(gx_size.bit_length() - 1)]
        for axis, flip in steps[:-1]:
            sums = sums + swapped(sums, axis, flip)
        other = swapped(sums, *steps[-1])
    else:
        sums = lax.psum(sums, ("gx", "gy"))
        other = jnp.zeros_like(sums)

    direct = ka_size == 4 and rows % (ROWS * ka_size) == 0
    slabs = ka_size if direct else 1
    slab = (planes, rows // slabs, lanes)
    slab_shapes = (slab, slab, (2,) + slab) if direct else (slab,)
    ritz, *pieces = pl.pallas_call(
        make_combine_kernel(float(cell_count), slabs, chunks),
        out_shape=(pltpu.VMEM((1, bands), F32),)
        + tuple(pltpu.VMEM(shape, F32) for shape in slab_shapes),
        in_specs=[vmem] * (5 + len(chunks)),
        out_specs=(vmem,) * (1 + len(slab_shapes)),
        compiler_params=params,
        name="combine",
    )(*[in_vmem(v) for v in (weights, sums, other, grad, massd, *last_grads)])
    if direct:
        own, near, far = pieces
        arrived = swapped(far, "ka", 2)
        design = own + arrived[0] + swapped(near + arrived[1], "ka", 1)
    else:
        design = lax.psum_scatter(pieces[0], "ka", scatter_dimension=1, tiled=True)
    return (ritz, design)


def solution(mesh):
    in_specs = (
        P("ka", None, None, None, "gx", "gy", None),
        P("gx", "gy", None),
        P(),
        P(),
        P("ka"),
        P("ka", None, None, None),
        P("ka", None),
    )
    out_specs = (P("ka", None), P("gx", ("gy", "ka"), None))
    return jax.shard_map(
        on_device, mesh=mesh, in_specs=in_specs, out_specs=out_specs, check_vma=False
    )
```

```python
import math

import jax
import jax.numpy as jnp
import numpy as np
from jax import lax
from jax.experimental import pallas as pl
from jax.experimental.pallas import tpu as pltpu
from jax.sharding import PartitionSpec as P

QGRID = 8
PHASES = 3
COMPS = 3
ROWS = 16
F32 = jnp.float32
BF16 = jnp.bfloat16
EXACT = lax.Precision.HIGHEST
VMEM_LIMIT = 56 * 1024 * 1024

vmem = pl.BlockSpec(memory_space=pltpu.VMEM)
smem = pl.BlockSpec(memory_space=pltpu.SMEM)


def in_vmem(value):
    return pltpu.with_memory_space_constraint(value, pltpu.VMEM)


def passed_along(value, axis, by):
    devices = lax.axis_size(axis)
    return lax.ppermute(value, axis, [(i, (i + by) % devices) for i in range(devices)])


def swapped(value, axis, flip):
    devices = lax.axis_size(axis)
    return lax.ppermute(value, axis, [(i, i ^ flip) for i in range(devices)])


def is_power(count):
    return count & (count - 1) == 0


def grid_turn(digit):
    angles = np.arange(QGRID, dtype=np.float32) * np.float32(2.0 * math.pi / QGRID)
    cosine, sine = jnp.float32(1.0), jnp.float32(0.0)
    for at in range(1, QGRID):
        cosine = jnp.where(digit == at, jnp.float32(np.cos(angles[at])), cosine)
        sine = jnp.where(digit == at, jnp.float32(np.sin(angles[at])), sine)
    return cosine, sine


def bf16_parts(value):
    high = value.astype(BF16)
    rest = value - high.astype(F32)
    middle = rest.astype(BF16)
    low = (rest - middle.astype(F32)).astype(BF16)
    return [high, middle, low]


def spread_rotation(real_part, imag_part, rows):
    bands = real_part.shape[0]
    wide = 2 * bands * rows
    tall_at = lax.broadcasted_iota(jnp.int32, (wide, bands), 0) // rows % bands
    tall = (tall_at == lax.broadcasted_iota(jnp.int32, (wide, bands), 1)).astype(F32)
    flat_at = lax.broadcasted_iota(jnp.int32, (bands, wide), 1) // rows % bands
    flat = (flat_at == lax.broadcasted_iota(jnp.int32, (bands, wide), 0)).astype(F32)

    def grown(matrix):
        tall_part = lax.dot_general(
            tall, matrix, (((1,), (1,)), ((), ())), precision=EXACT, preferred_element_type=F32
        )
        return jnp.dot(tall_part, flat, precision=EXACT, preferred_element_type=F32)

    row_at = lax.broadcasted_iota(jnp.int32, (wide, wide), 0)
    column_at = lax.broadcasted_iota(jnp.int32, (wide, wide), 1)
    row_half = row_at // (bands * rows)
    column_half = column_at // (bands * rows)
    real_grown = grown(real_part)
    imag_grown = grown(imag_part)
    imag_grown = jnp.where(row_half > column_half, imag_grown, -imag_grown)
    full = jnp.where(row_half == column_half, real_grown, imag_grown)
    full = jnp.where(row_at % rows == column_at % rows, full, 0.0)
    return jnp.concatenate(bf16_parts(full), axis=1)


def write_spread(out_ref, real_part, imag_part):
    bands = real_part.shape[0]
    half = bands * ROWS
    tall_at = lax.broadcasted_iota(jnp.int32, (half, bands), 0) // ROWS
    tall = (tall_at == lax.broadcasted_iota(jnp.int32, (half, bands), 1)).astype(BF16)
    flat_at = lax.broadcasted_iota(jnp.int32, (bands, half), 1) // ROWS
    flat = (flat_at == lax.broadcasted_iota(jnp.int32, (bands, half), 0)).astype(BF16)
    same_row = (lax.broadcasted_iota(jnp.int32, (half, half), 0) % ROWS) == (
        lax.broadcasted_iota(jnp.int32, (half, half), 1) % ROWS
    )

    def grown(part):
        tall_part = lax.dot_general(
            tall, part, (((1,), (1,)), ((), ())), preferred_element_type=F32
        ).astype(BF16)
        return jnp.where(same_row, jnp.dot(tall_part, flat, preferred_element_type=F32), 0.0)

    parts = zip(bf16_parts(real_part), bf16_parts(imag_part))
    for at, (real_bf16, imag_bf16) in enumerate(parts):
        real_grown, imag_grown = grown(real_bf16), grown(imag_bf16)
        left = slice(2 * at * half, (2 * at + 1) * half)
        right = slice((2 * at + 1) * half, (2 * at + 2) * half)
        out_ref[0:half, left] = real_grown.astype(BF16)
        out_ref[0:half, right] = (-imag_grown).astype(BF16)
        out_ref[half : 2 * half, left] = imag_grown.astype(BF16)
        out_ref[half : 2 * half, right] = real_grown.astype(BF16)


def row_chunks(rows):
    tiles = rows // ROWS
    sizes = [tiles - 1, 1] if tiles > 1 else [1]
    chunks, begin = [], 0
    for size in sizes:
        chunks.append((begin, size * ROWS))
        begin += size * ROWS
    return chunks


def turned_parts(real_part, imag_part, cosine, sine):
    return cosine * real_part - sine * imag_part, sine * real_part + cosine * imag_part


def picked(table, column, label_block):
    low = jnp.where(label_block == 0, table[0, column], table[1, column])
    return jnp.where(label_block == 2, table[2, column], low)


def rows_to_lanes(column, lanes):
    shape = (column.shape[0], lanes)
    diagonal = lax.broadcasted_iota(jnp.int32, shape, 0) == lax.broadcasted_iota(jnp.int32, shape, 1)
    return jnp.sum(jnp.where(diagonal, column, 0.0), axis=0, keepdims=True)


def lanes_to_rows(row, count):
    shape = (count, row.shape[1])
    diagonal = lax.broadcasted_iota(jnp.int32, shape, 0) == lax.broadcasted_iota(jnp.int32, shape, 1)
    return jnp.sum(jnp.where(diagonal, row, 0.0), axis=1, keepdims=True)


def make_slice_kernel(begin, size, in_steps):
    def slice_kernel(u_ref, *refs):
        out_ref, sem = refs[-2:]
        source = u_ref.at[0, :, :, :, 0, begin : begin + size]
        whole = pltpu.make_async_copy(source, out_ref, sem)
        if not in_steps:
            whole.start()
            whole.wait()
            return
        second = lax.axis_index("ka") % 2 == 1

        @pl.when(jnp.logical_not(second))
        def _():
            whole.start()
            whole.wait()

        @pl.when(second)
        def _():
            for comp in range(COMPS):
                for first in range(0, size, ROWS):
                    here = (slice(None), comp, slice(None), slice(first, first + ROWS))
                    piece = pltpu.make_async_copy(source.at[here], out_ref.at[here], sem)
                    piece.start()
                    piece.wait()

    return slice_kernel


def edge_row_kernel(u_ref, after_ref, out_ref):
    planes = u_ref.shape[4]
    for comp in range(COMPS):
        for plane in range(planes):
            tile = u_ref[0, :, comp, :, plane, :, :].astype(F32)
            rows = tile.reshape(tile.shape[0] * tile.shape[1], ROWS, tile.shape[3])[:, 0, :]
            out_ref[comp, plane] = rows.astype(BF16)


def interior_kernel(
    kpoint_ref,
    props_ref,
    slopes_ref,
    weights_in_ref,
    rotation_ref,
    labels_ref,
    u_ref,
    yrow_ref,
    spread_ref,
    last_modes_ref,
    grad_ref,
    massd_ref,
    strain_ref,
    dil_ref,
    sums_ref,
    mats_ref,
    weights_ref,
    modes_ref,
    acc_ref,
    own_ref,
):
    planes, rows, lanes = labels_ref.shape
    bands = u_ref.shape[3]
    channels = 2 * bands
    q_index = kpoint_ref[0, 0]
    band_at = lax.broadcasted_iota(jnp.int32, (bands, lanes), 0)
    weights = jnp.zeros((bands, lanes), F32)
    for band in range(bands):
        weights = jnp.where(band_at == band, weights_in_ref[0, band], weights)
    weights_ref[...] = weights
    x_last = lax.axis_index("gx") == lax.axis_size("gx") - 1
    y_last = lax.axis_index("gy") == lax.axis_size("gy") - 1
    x_turn = grid_turn(jnp.where(x_last, q_index // (QGRID * QGRID), 0))
    y_turn = grid_turn(jnp.where(y_last, q_index // QGRID % QGRID, 0))
    z_turn = grid_turn(q_index % QGRID)
    real_part, imag_part = rotation_ref[0, 0], rotation_ref[0, 1]
    write_spread(own_ref, real_part, imag_part)
    write_spread(spread_ref, *turned_parts(real_part, imag_part, *x_turn))
    spread_own = own_ref[...]
    edge_mix = spread_rotation(*turned_parts(real_part, imag_part, *y_turn), 1)
    for tile in range(rows // ROWS):
        here = slice(tile * ROWS, (tile + 1) * ROWS)
        for comp in range(COMPS):
            source = jnp.concatenate(
                [
                    u_ref[0, :, comp, :, plane, here, :].reshape(channels * ROWS, lanes)
                    for plane in range(planes)
                ],
                axis=1,
            )
            source = jnp.concatenate([source] * 3, axis=0)
            turned = jnp.dot(spread_own, source, preferred_element_type=F32)
            for plane in range(planes):
                part = turned[:, plane * lanes : (plane + 1) * lanes]
                part = part.reshape(channels, ROWS, lanes)
                modes_ref[plane, comp, :, here, :] = part
                if plane == planes - 1:
                    last_modes_ref[comp, :, here, :] = part
    for plane in range(planes):
        for comp in range(COMPS):
            edge = yrow_ref[comp, plane]
            edge = jnp.concatenate([edge] * 3, axis=0)
            edge = jnp.dot(edge_mix, edge, preferred_element_type=F32)
            modes_ref[plane, comp, :, rows : rows + 1, :] = edge[:, None, :]
        for column in range(3):
            mats_ref[column, plane] = picked(props_ref, column, labels_ref[plane])
            mats_ref[3 + column, plane] = picked(slopes_ref, column, labels_ref[plane])
    lane_at = lax.broadcasted_iota(jnp.int32, (ROWS, lanes), 1)
    is_end = lane_at == lanes - 1
    turn_cos = jnp.where(is_end, z_turn[0], 1.0)
    turn_sin = jnp.where(is_end, z_turn[1], 0.0)

    def per_band(band, carry):
        for plane in range(planes):
            inner = plane < planes - 1
            mass_sum = jnp.zeros((ROWS, lanes), F32)
            stiff_sum = jnp.zeros((ROWS, lanes), F32)
            for tile in range(rows // ROWS):
                begin = tile * ROWS
                here = slice(begin, begin + ROWS)
                after = slice(begin + 1, begin + 1 + ROWS)
                strain_sq = jnp.zeros((ROWS, lanes), F32)
                mass_sq = jnp.zeros((ROWS, lanes), F32)
                dil = [jnp.zeros((ROWS, lanes), F32)] * 2
                for comp in range(COMPS):
                    own = [modes_ref[plane, comp, t * bands + band, here, :] for t in range(2)]
                    roll = [pltpu.roll(v, lanes - 1, 1) for v in own]
                    along_z = [
                        turn_cos * roll[0] - turn_sin * roll[1],
                        turn_sin * roll[0] + turn_cos * roll[1],
                    ]
                    for t in range(2):
                        diff_z = along_z[t] - own[t]
                        diff_y = modes_ref[plane, comp, t * bands + band, after, :] - own[t]
                        strain_sq = strain_sq + diff_z * diff_z + diff_y * diff_y
                        if inner:
                            diff_x = (
                                modes_ref[plane + 1, comp, t * bands + band, here, :] - own[t]
                            )
                            strain_sq = strain_sq + diff_x * diff_x
                            if comp == 0:
                                dil[t] = dil[t] + diff_x
                        if comp == 1:
                            dil[t] = dil[t] + diff_y
                        if comp == 2:
                            dil[t] = dil[t] + diff_z
                        mass_sq = mass_sq + own[t] * own[t]
                mass_sum = mass_sum + mats_ref[2, plane, here, :] * mass_sq
                massd_ref[band, plane, here, :] = mats_ref[5, plane, here, :] * mass_sq
                if inner:
                    dil_sq = dil[0] * dil[0] + dil[1] * dil[1]
                    stiff_sum = (
                        stiff_sum
                        + mats_ref[0, plane, here, :] * strain_sq
                        + mats_ref[1, plane, here, :] * dil_sq
                    )
                    grad_ref[band, plane, here, :] = (
                        mats_ref[3, plane, here, :] * strain_sq
                        + mats_ref[4, plane, here, :] * dil_sq
                    )
                else:
                    strain_ref[band, here, :] = strain_sq
                    dil_ref[0, band, here, :] = dil[0]
                    dil_ref[1, band, here, :] = dil[1]
            acc_ref[plane, band] = stiff_sum
            acc_ref[planes + plane, band] = mass_sum
        return carry

    lax.fori_loop(0, bands, per_band, 0)
    sums_ref[0:bands] = jnp.sum(jnp.sum(acc_ref[0:planes], axis=0), axis=1)
    sums_ref[bands : 2 * bands] = jnp.sum(jnp.sum(acc_ref[planes : 2 * planes], axis=0), axis=1)


def make_edge_kernel(begin, size, last):
    def edge_kernel(
        mats_ref,
        spread_ref,
        modes_ref,
        strain_ref,
        dil_ref,
        sums_in_ref,
        plane_ref,
        grad_ref,
        sums_ref,
        next_ref,
        acc_ref,
    ):
        bands, _, lanes = strain_ref.shape
        channels = 2 * bands
        tiles = size // ROWS
        blocks = [(comp, tile) for comp in range(COMPS) for tile in range(tiles)]
        source = jnp.concatenate(
            [
                plane_ref[:, comp, :, tile * ROWS : (tile + 1) * ROWS, :].reshape(
                    channels * ROWS, lanes
                )
                for comp, tile in blocks
            ],
            axis=1,
        )
        source = jnp.concatenate([source] * 3, axis=0)
        turned = jnp.dot(spread_ref[...], source, preferred_element_type=F32)
        for at, (comp, tile) in enumerate(blocks):
            next_ref[comp, :, tile * ROWS : (tile + 1) * ROWS, :] = turned[
                :, at * lanes : (at + 1) * lanes
            ].reshape(channels, ROWS, lanes)
        plane = mats_ref.shape[1] - 1
        for band in range(bands):
            stiff_sum = jnp.zeros((ROWS, lanes), F32)
            for tile in range(tiles):
                here = slice(begin + tile * ROWS, begin + (tile + 1) * ROWS)
                there = slice(tile * ROWS, (tile + 1) * ROWS)
                strain_sq = strain_ref[band, here, :]
                dil = [dil_ref[t, band, here, :] for t in range(2)]
                for comp in range(COMPS):
                    for t in range(2):
                        diff_x = (
                            next_ref[comp, t * bands + band, there, :]
                            - modes_ref[comp, t * bands + band, here, :]
                        )
                        strain_sq = strain_sq + diff_x * diff_x
                        if comp == 0:
                            dil[t] = dil[t] + diff_x
                dil_sq = dil[0] * dil[0] + dil[1] * dil[1]
                grad_ref[band, there, :] = (
                    mats_ref[3, plane, here, :] * strain_sq + mats_ref[4, plane, here, :] * dil_sq
                )
                stiff_sum = (
                    stiff_sum
                    + mats_ref[0, plane, here, :] * strain_sq
                    + mats_ref[1, plane, here, :] * dil_sq
                )
            acc_ref[band : band + 1] = sums_in_ref[band : band + 1] + jnp.sum(
                stiff_sum, axis=0, keepdims=True
            )
        acc_ref[bands : 2 * bands] = sums_in_ref[bands : 2 * bands]
        if last:
            sums_ref[...] = rows_to_lanes(jnp.sum(acc_ref[...], axis=1, keepdims=True), lanes)
        else:
            sums_ref[...] = acc_ref[...]

    return edge_kernel


def make_combine_kernel(cell_count, slabs, chunks):
    def combine_kernel(weights_ref, sums_a_ref, sums_b_ref, grad_ref, massd_ref, *refs):
        last_grad_refs = refs[: len(chunks)]
        ritz_ref, slab_refs = refs[len(chunks)], refs[len(chunks) + 1 :]
        bands, planes, rows, lanes = massd_ref.shape
        sums = sums_a_ref[...] + sums_b_ref[...]
        sums = jnp.broadcast_to(lanes_to_rows(sums, 2 * bands), (2 * bands, lanes))
        stiff = sums[0:bands]
        inert = sums[bands : 2 * bands]
        ritz = stiff / inert
        factor = weights_ref[...] * (cell_count / inert)
        tail = factor * ritz
        ritz_ref[...] = rows_to_lanes(ritz, lanes)[:, 0:bands]
        tiles = rows // ROWS // slabs
        me = lax.axis_index("ka") if slabs > 1 else 0
        for plane in range(planes):
            totals = []
            for begin in range(0, rows, ROWS):
                here = slice(begin, begin + ROWS)
                part = [i for i, (first, size) in enumerate(chunks) if first <= begin < first + size][0]
                there = slice(begin - chunks[part][0], begin - chunks[part][0] + ROWS)
                total = jnp.zeros((ROWS, lanes), F32)
                for band in range(bands):
                    if plane < planes - 1:
                        term = grad_ref[band, plane, here, :]
                    else:
                        term = last_grad_refs[part][band, there, :]
                    total = total + factor[band : band + 1] * term
                    total = total - tail[band : band + 1] * massd_ref[band, plane, here, :]
                totals.append(total)
            for at in range(slabs):
                for tile in range(tiles):
                    value = totals[at * tiles + tile]
                    for other in range(1, slabs):
                        value = jnp.where(me == other, totals[(at ^ other) * tiles + tile], value)
                    there = slice(tile * ROWS, (tile + 1) * ROWS)
                    if at >= 2:
                        slab_refs[2][at - 2, plane, there, :] = value
                    else:
                        slab_refs[at][plane, there, :] = value

    return combine_kernel


def on_device(band_fields, labels, phase_props, slopes, kpoints, rotations, band_weights):
    planes, rows, lanes = labels.shape
    bands = band_fields.shape[3]
    channels = 2 * bands
    gx_size = lax.axis_size("gx")
    gy_size = lax.axis_size("gy")
    ka_size = lax.axis_size("ka")
    cell_count = gx_size * gy_size * planes * rows * lanes
    params = pltpu.CompilerParams(vmem_limit_bytes=VMEM_LIMIT)

    chunks = row_chunks(rows)
    sliced, yrow = [], None
    for begin, size in chunks:
        behind = sliced[-1:] if yrow is None or len(sliced) > 1 else [yrow]
        sliced.append(
            pl.pallas_call(
                make_slice_kernel(begin, size, not sliced),
                out_shape=pltpu.VMEM((2, COMPS, bands, size, lanes), BF16),
                in_specs=[pl.BlockSpec(memory_space=pl.ANY)] + [vmem] * len(behind),
                out_specs=vmem,
                scratch_shapes=[pltpu.SemaphoreType.DMA(())],
                compiler_params=params,
                name="slice",
            )(band_fields, *[in_vmem(v) for v in behind])
        )
        if yrow is None:
            yrow = pl.pallas_call(
                edge_row_kernel,
                out_shape=pltpu.VMEM((COMPS, planes, channels, lanes), BF16),
                in_specs=[
                    pl.BlockSpec(
                        (1, 2, COMPS, bands, planes, ROWS, lanes), lambda i: (0, 0, 0, 0, 0, 0, 0)
                    ),
                    vmem,
                ],
                out_specs=pl.BlockSpec((COMPS, planes, channels, lanes), lambda i: (0, 0, 0, 0)),
                grid=(1,),
                compiler_params=params,
                name="edge_row",
            )(band_fields, in_vmem(sliced[0]))
    xplanes = [passed_along(value, "gx", -1) for value in sliced]
    yrow = passed_along(yrow, "gy", -1)

    spread, last_modes, grad, massd, strain, dil, sums, mats, weights = pl.pallas_call(
        interior_kernel,
        out_shape=(
            pltpu.VMEM((channels * ROWS, 3 * channels * ROWS), BF16),
            pltpu.VMEM((COMPS, channels, rows, lanes), F32),
            pltpu.VMEM((bands, planes - 1, rows, lanes), F32),
            pltpu.VMEM((bands, planes, rows, lanes), F32),
            pltpu.VMEM((bands, rows, lanes), F32),
            pltpu.VMEM((2, bands, rows, lanes), F32),
            pltpu.VMEM((2 * bands, lanes), F32),
            pltpu.VMEM((6, planes, rows, lanes), F32),
            pltpu.VMEM((bands, lanes), F32),
        ),
        in_specs=[smem, smem, smem, smem, vmem, vmem, vmem, vmem],
        out_specs=(vmem,) * 9,
        scratch_shapes=[
            pltpu.VMEM((planes, COMPS, channels, rows + 8, lanes), F32),
            pltpu.VMEM((2 * planes, bands, ROWS, lanes), F32),
            pltpu.VMEM((channels * ROWS, 3 * channels * ROWS), BF16),
        ],
        compiler_params=params,
        name="interior",
    )(kpoints.reshape(1, 1), phase_props, slopes, band_weights, rotations, labels, band_fields, in_vmem(yrow))

    last_grads = []
    for (begin, size), xplane in zip(chunks, xplanes):
        last = len(last_grads) == len(chunks) - 1
        last_grad, sums = pl.pallas_call(
            make_edge_kernel(begin, size, last),
            out_shape=(
                pltpu.VMEM((bands, size, lanes), F32),
                pltpu.VMEM((1 if last else 2 * bands, lanes), F32),
            ),
            in_specs=[vmem] * 7,
            out_specs=(vmem, vmem),
            scratch_shapes=[
                pltpu.VMEM((COMPS, channels, size, lanes), F32),
                pltpu.VMEM((2 * bands, lanes), F32),
            ],
            compiler_params=params,
            name="edge",
        )(*[in_vmem(v) for v in (mats, spread, last_modes, strain, dil, sums, xplane)])
        last_grads.append(last_grad)

    if is_power(gx_size) and is_power(gy_size) and gx_size > 1:
        steps = [("gy", 1 << i) for i in range(gy_size.bit_length() - 1)]
        steps += [("gx", 1 << i) for i in range(gx_size.bit_length() - 1)]
        for axis, flip in steps[:-1]:
            sums = sums + swapped(sums, axis, flip)
        other = swapped(sums, *steps[-1])
    else:
        sums = lax.psum(sums, ("gx", "gy"))
        other = jnp.zeros_like(sums)

    direct = ka_size == 4 and rows % (ROWS * ka_size) == 0
    slabs = ka_size if direct else 1
    slab = (planes, rows // slabs, lanes)
    slab_shapes = (slab, slab, (2,) + slab) if direct else (slab,)
    ritz, *pieces = pl.pallas_call(
        make_combine_kernel(float(cell_count), slabs, chunks),
        out_shape=(pltpu.VMEM((1, bands), F32),)
        + tuple(pltpu.VMEM(shape, F32) for shape in slab_shapes),
        in_specs=[vmem] * (5 + len(chunks)),
        out_specs=(vmem,) * (1 + len(slab_shapes)),
        compiler_params=params,
        name="combine",
    )(*[in_vmem(v) for v in (weights, sums, other, grad, massd, *last_grads)])
    if direct:
        own, near, far = pieces
        arrived = swapped(far, "ka", 2)
        design = own + arrived[0] + swapped(near + arrived[1], "ka", 1)
    else:
        design = lax.psum_scatter(pieces[0], "ka", scatter_dimension=1, tiled=True)
    return (ritz, design)


def solution(mesh):
    in_specs = (
        P("ka", None, None, None, "gx", "gy", None),
        P("gx", "gy", None),
        P(),
        P(),
        P("ka"),
        P("ka", None, None, None),
        P("ka", None),
    )
    out_specs = (P("ka", None), P("gx", ("gy", "ka"), None))
    return jax.shard_map(
        on_device, mesh=mesh, in_specs=in_specs, out_specs=out_specs, check_vma=False
    )
```
